128 devices in a mesh: section: 4 (over y), fsdp: 32 (over x, z, core).
Axes of the slice: x: 4, y: 4, z: 4, core: 2. Of those that a mesh axis runs over, the one named last changes fastest.
Arguments:
- inputs: bfloat16 [3, 128, 3072], P(None, 'fsdp'), may hold values from -6 to 6
- gain: float32 [4, 3072], P('section'), may hold values from 0.25 to 1.75
- w_gate: bfloat16 [4, 4, 3072, 8192], P('section', None, None, 'fsdp'), may hold values from -0.109375 to 0.109375
- w_up: bfloat16 [4, 4, 3072, 8192], P('section', None, None, 'fsdp'), may hold values from -0.109375 to 0.109375
- w_down: bfloat16 [4, 4, 8192, 3072], P('section', None, 'fsdp'), may hold values from -0.0625 to 0.0625
- routes: int32 [4, 3, 128, 2], P('section'), may hold values from 0 to 3, all different within a row
- shares: float32 [4, 3, 128, 2], P('section'), may hold values from 0.1 to 1
Outputs:
- hidden: bfloat16 [4, 3, 128, 3072], P('section', None, 'fsdp')
The draws below stay inside these ranges and needn't reach their ends.
Inputs may be any that keep to these rules, and one draw needn't show every extreme that they name: `routes`: each token names 2 different experts, and every expert is named in each microbatch of each layer.
All inputs are finite; a program needn't handle non-finite values.
Results may differ from the reference program's by a relative error of at most 0.014.
Values may be sent and summed in bfloat16 or wider, within the bound.
A program may use at most 128 MiB of HBM per device.

```python
import math
import jax
import jax.numpy as jnp
from jax import lax

D = 3072
FF = 8192
E = 4
TOP = 2
BLOCK = 128
MICRO = 3
LAYERS = 4
TOKENS = 128


def block_scale(stream_key, extent, cuts, smallest, high):
    def one(dim, blocks):
        draws = jax.random.uniform(jax.random.fold_in(jax.random.fold_in(stream_key, 6), dim), (blocks,), jnp.float32, smallest / len(cuts), high / len(cuts))
        return jnp.repeat(jnp.exp(draws), extent[dim] // blocks).reshape((-1,) + (1,) * (len(extent) - dim - 1))

    loudness = one(*cuts[0])
    for cut in cuts[1:]:
        loudness = loudness * one(*cut)
    return loudness


def distinct(key, rows, number_of, top, lift):
    sequence = jax.random.permutation(jax.random.fold_in(key, 1), number_of)
    favour = sequence
    for power in range(3):
        favour = favour * favour // number_of
    favour = favour * lift // number_of
    chance = jax.random.randint(jax.random.fold_in(key, 2), (rows, number_of), 0, 4096) + favour
    fixed_rows = jax.random.permutation(jax.random.fold_in(key, 3), rows)[jnp.arange(number_of) % rows]
    chance = jnp.where(jnp.arange(rows)[:, None] == fixed_rows[None, :], 1 << 14, chance)
    priority = chance * number_of + jnp.arange(number_of)
    return lax.top_k(priority.astype(jnp.int32), top)[1].astype(jnp.int32)


def gaussian(rng, extent, deviation, limit, pieces=(), kind=jnp.bfloat16):
    array = jax.random.normal(rng, extent, jnp.float32) * deviation
    if len(pieces) > 0:
        array = block_scale(rng, extent, pieces, -0.22, 0.18) * array
    return jnp.clip(array, min=-limit, max=limit).astype(kind)


def setup_inputs(seed: int = 0) -> dict:
    streams_of = jax.random.split(jax.random.key(seed), 8)
    inputs = gaussian(streams_of[0], (MICRO, TOKENS, D), 1.0, 6.0, ((1, 32),))
    gain = jnp.clip(1.0 + 0.15 * jax.random.normal(streams_of[1], (LAYERS, D), jnp.float32), 0.25, 1.75)
    w_gate = gaussian(streams_of[2], (LAYERS, E, D, FF), D ** -0.5, 0.109375, ((0, 4), (3, 32)))
    w_up = gaussian(streams_of[3], (LAYERS, E, D, FF), D ** -0.5, 0.109375, ((0, 4), (3, 32)))
    w_down = gaussian(streams_of[4], (LAYERS, E, FF, D), FF ** -0.5, 0.0625, ((0, 4), (2, 32)))
    routes = distinct(streams_of[5], LAYERS * MICRO * TOKENS, E, TOP, 8192).reshape((LAYERS, MICRO, TOKENS, TOP))
    shares = jnp.clip(jnp.exp(math.log(1.0) - 2.3025851 * jax.random.uniform(streams_of[6], (LAYERS, MICRO, TOKENS, TOP), jnp.float32) ** block_scale(streams_of[6], (LAYERS, MICRO, TOKENS, TOP), ((0, 4),), -0.2, 0.2)), 0.1, 1.0)
    return {"inputs": inputs, "gain": gain, "w_gate": w_gate, "w_up": w_up, "w_down": w_down, "routes": routes, "shares": shares}


def arrange(choices, experts, block, nblocks):
    flat_choice = choices.reshape(-1).astype(jnp.int32)
    slots_used = flat_choice.shape[0]
    onehot = (flat_choice[:, None] == jnp.arange(experts, dtype=jnp.int32)[None, :]).astype(jnp.int32)
    counts = lax.optimization_barrier(jnp.sum(onehot, axis=0))
    padded = (counts + block - 1) // block * block
    ends = jnp.cumsum(padded).astype(jnp.int32)
    starts = ends - padded
    before = jnp.cumsum(onehot, axis=0) - onehot
    destination = lax.optimization_barrier(jnp.sum((before + starts[None, :]) * onehot, axis=1)).astype(jnp.int32)
    source = jnp.zeros((nblocks * block,), jnp.int32).at[destination].set(jnp.arange(slots_used, dtype=jnp.int32))
    slot_live = jnp.zeros((nblocks * block,), jnp.int32).at[destination].set(1)
    block_first = jnp.arange(nblocks, dtype=jnp.int32) * block
    block_expert = jnp.minimum(lax.optimization_barrier(jnp.sum((block_first[:, None] >= ends[None, :]).astype(jnp.int32), axis=1)), experts - 1).astype(jnp.int32)
    block_live = block_first < ends[experts - 1]
    return (destination, source, slot_live, block_expert, block_live)

def expert_mix(normed, choices, weights_share, gate_w, up_w, down_w):
    tokens, width = normed.shape
    experts = gate_w.shape[0]
    nblocks = (2 * tokens + BLOCK - 1) // BLOCK + experts
    destination, source, slot_live, block_expert, block_live = arrange(choices, experts, BLOCK, nblocks)
    picked_rows = jnp.where(slot_live[:, None] > 0, normed[source // 2], jnp.zeros((), normed.dtype))
    blocks = picked_rows.reshape(nblocks, BLOCK, width)

    def one_block(item):
        rows_block, expert_id, live = item

        def compute(operand):
            gate = jnp.dot(operand, gate_w[expert_id], preferred_element_type=jnp.float32)
            upward = jnp.dot(operand, up_w[expert_id], preferred_element_type=jnp.float32)
            gated = (jax.nn.silu(gate) * upward).astype(jnp.bfloat16)
            return jnp.dot(gated, down_w[expert_id], preferred_element_type=jnp.float32)

        def nothing(operand):
            return jnp.zeros((operand.shape[0], down_w.shape[2]), jnp.float32)
        return lax.cond(live, compute, nothing, rows_block)
    results = lax.map(one_block, (blocks, block_expert, block_live))
    results = results.reshape(nblocks * BLOCK, width)
    chosen = results[destination].reshape(tokens, 2, width)
    return lax.optimization_barrier(jnp.sum(chosen * weights_share[:, :, None].astype(jnp.float32), axis=1))

def rms_norm(rows, gain_row):
    values = rows.astype(jnp.float32)
    scale = lax.rsqrt(lax.optimization_barrier(jnp.mean(values * values, axis=-1, keepdims=True)) + 1e-05)
    return (values * scale * gain_row[None, :]).astype(jnp.bfloat16)

def reference(inputs, gain, w_gate, w_up, w_down, routes, shares):

    def layer(state, params):
        gain_row, gate_w, up_w, down_w, route_layer, share_layer = params

        def one_micro(item):
            rows, route_micro, share_micro = item
            normed = rms_norm(rows, gain_row)
            mixed = expert_mix(normed, route_micro, share_micro, gate_w, up_w, down_w)
            return (rows.astype(jnp.float32) + mixed).astype(jnp.bfloat16)
        result = lax.map(one_micro, (state, route_layer, share_layer))
        return (result, result)
    _, outputs = lax.scan(layer, inputs, (gain, w_gate, w_up, w_down, routes, shares))
    return outputs
```

```python
import jax
import jax.numpy as jnp
from jax import lax
from jax.sharding import PartitionSpec as P


def passed_along(array, axis, by):
    devices = lax.axis_size(axis)
    pairs = [(i, i + by) for i in range(devices) if 0 <= i + by < devices]
    return lax.ppermute(array, axis, pairs)


def rms_norm(rows, gain_row):
    values = rows.astype(jnp.float32)
    scale = lax.rsqrt(jnp.mean(values * values, axis=-1, keepdims=True) + 1e-05)
    return (values * scale * gain_row[None, :]).astype(jnp.bfloat16)


def combine_weights(route_layer, share_layer, experts, shards):
    micro, tokens, top = route_layer.shape
    per = tokens // shards
    onehot = (route_layer[..., None] == jnp.arange(experts, dtype=route_layer.dtype)).astype(jnp.float32)
    coef = jnp.sum(onehot * share_layer[..., None], axis=2)
    coef = coef.reshape(micro, shards, per, experts).transpose(3, 1, 0, 2)
    return coef.reshape(experts, shards, micro * per)


def expert_mix(rows, coef, gate_w, up_w, down_w):
    gate = jnp.einsum("fmd,edh->efmh", rows, gate_w, preferred_element_type=jnp.float32)
    upward = jnp.einsum("fmd,edh->efmh", rows, up_w, preferred_element_type=jnp.float32)
    gated = (jax.nn.silu(gate) * upward * coef[..., None]).astype(jnp.bfloat16)
    return jnp.einsum("efmh,ehd->fmd", gated, down_w, preferred_element_type=jnp.float32)


def on_device(inputs, gain, w_gate, w_up, w_down, routes, shares):
    sections = lax.axis_size("section")
    shards = lax.axis_size("fsdp")
    section_index = lax.axis_index("section")
    micro, local, width = inputs.shape
    gain_row = gain[0]
    gate_w, up_w, down_w = w_gate[0], w_up[0], w_down[0]
    coef = combine_weights(routes[0], shares[0], gate_w.shape[0], shards)
    current = inputs.reshape(micro * local, width)
    output = jnp.zeros_like(current)
    for tick in range(sections):
        if tick > 0:
            current = passed_along(result, "section", 1)
        normed = rms_norm(current, gain_row)
        gathered = lax.all_gather(normed, "fsdp", axis=0, tiled=False)
        partial_value = expert_mix(gathered, coef, gate_w, up_w, down_w)
        mixed = lax.psum_scatter(partial_value, "fsdp", scatter_dimension=0, tiled=True)[0]
        result = (current.astype(jnp.float32) + mixed).astype(jnp.bfloat16)
        output = jnp.where(section_index == tick, result, output)
    return output.reshape(1, micro, local, width)


def solution(mesh):
    placed = (
        P(None, "fsdp", None),
        P("section", None),
        P("section", None, None, "fsdp"),
        P("section", None, None, "fsdp"),
        P("section", None, "fsdp", None),
        P("section", None, None, None),
        P("section", None, None, None),
    )
    return jax.shard_map(
        on_device,
        mesh=mesh,
        in_specs=placed,
        out_specs=P("section", None, "fsdp", None),
        check_vma=False,
    )
```

```python
import jax
import jax.numpy as jnp
from jax import lax
from jax.sharding import PartitionSpec as P


def passed_along(array, axis, by):
    devices = lax.axis_size(axis)
    pairs = [(i, i + by) for i in range(devices) if 0 <= i + by < devices]
    return lax.ppermute(array, axis, pairs)


def rms_norm(rows, gain_row):
    values = rows.astype(jnp.float32)
    scale = lax.rsqrt(jnp.mean(values * values, axis=-1, keepdims=True) + 1e-05)
    return (values * scale * gain_row[None, :]).astype(jnp.bfloat16)


def combine_weights(route_layer, share_layer, experts, shards):
    micro, tokens, top = route_layer.shape
    per = tokens // shards
    onehot = (route_layer[..., None] == jnp.arange(experts, dtype=route_layer.dtype)).astype(jnp.float32)
    coef = jnp.sum(onehot * share_layer[..., None], axis=2)
    coef = coef.reshape(micro, shards, per, experts).transpose(3, 1, 0, 2)
    return coef.reshape(experts, shards, micro * per)


def expert_mix(rows, coef, gate_w, up_w, down_w):
    gate = jnp.einsum("fmd,edh->efmh", rows, gate_w, preferred_element_type=jnp.float32)
    upward = jnp.einsum("fmd,edh->efmh", rows, up_w, preferred_element_type=jnp.float32)
    gated = (jax.nn.silu(gate) * upward * coef[..., None]).astype(jnp.bfloat16)
    return jnp.einsum("efmh,ehd->fmd", gated, down_w, preferred_element_type=jnp.float32)


def on_device(inputs, gain, w_gate, w_up, w_down, routes, shares):
    sections = lax.axis_size("section")
    shards = lax.axis_size("fsdp")
    section_index = lax.axis_index("section")
    micro, local, width = inputs.shape
    gain_row = gain[0]
    gate_w, up_w, down_w = w_gate[0], w_up[0], w_down[0]
    coef = combine_weights(routes[0], shares[0], gate_w.shape[0], shards)
    current = inputs.reshape(micro * local, width)
    output = jnp.zeros_like(current)
    for tick in range(sections):
        if tick > 0:
            current = passed_along(result, "section", 1)
        normed = rms_norm(current, gain_row)
        spread = jnp.broadcast_to(normed[None], (shards,) + normed.shape)
        gathered = lax.all_to_all(spread, "fsdp", 0, 0, tiled=True)
        partial_value = expert_mix(gathered, coef, gate_w, up_w, down_w)
        pieces = lax.all_to_all(partial_value, "fsdp", 0, 0, tiled=True)
        mixed = jnp.sum(pieces, axis=0)
        result = (current.astype(jnp.float32) + mixed).astype(jnp.bfloat16)
        output = jnp.where(section_index == tick, result, output)
    return output.reshape(1, micro, local, width)


def solution(mesh):
    placed = (
        P(None, "fsdp", None),
        P("section", None),
        P("section", None, None, "fsdp"),
        P("section", None, None, "fsdp"),
        P("section", None, "fsdp", None),
        P("section", None, None, None),
        P("section", None, None, None),
    )
    return jax.shard_map(
        on_device,
        mesh=mesh,
        in_specs=placed,
        out_specs=P("section", None, "fsdp", None),
        check_vma=False,
    )
```

```python
import jax
import jax.numpy as jnp
from jax import lax
from jax.sharding import PartitionSpec as P


def passed_along(array, axis, by):
    devices = lax.axis_size(axis)
    pairs = [(i, i + by) for i in range(devices) if 0 <= i + by < devices]
    return lax.ppermute(array, axis, pairs)


def sibling(array, axis):
    devices = lax.axis_size(axis)
    return lax.ppermute(array, axis, [(i, i ^ 1) for i in range(devices)])


def rms_norm(rows, gain_row):
    values = rows.astype(jnp.float32)
    scale = lax.rsqrt(jnp.mean(values * values, axis=-1, keepdims=True) + 1e-05)
    return (values * scale * gain_row[None, :]).astype(jnp.bfloat16)


def combine_weights(route_layer, share_layer, experts, shards):
    micro, tokens, top = route_layer.shape
    per = tokens // shards
    onehot = (route_layer[..., None] == jnp.arange(experts, dtype=route_layer.dtype)).astype(jnp.float32)
    coef = jnp.sum(onehot * share_layer[..., None], axis=2)
    coef = coef.reshape(micro, shards, per, experts).transpose(3, 1, 0, 2)
    return coef.reshape(experts, shards, micro * per)


def expert_mix(rows, coef, gate_w, up_w, down_w):
    gate = jnp.einsum("fmd,edh->efmh", rows, gate_w, preferred_element_type=jnp.float32)
    upward = jnp.einsum("fmd,edh->efmh", rows, up_w, preferred_element_type=jnp.float32)
    gated = (jax.nn.silu(gate) * upward * coef[..., None]).astype(jnp.bfloat16)
    return jnp.einsum("efmh,ehd->fmd", gated, down_w, preferred_element_type=jnp.float32)


def on_device(inputs, gain, w_gate, w_up, w_down, routes, shares):
    sections = lax.axis_size("section")
    shards = lax.axis_size("fsdp")
    chips = shards // 2
    section_index = lax.axis_index("section")
    core = lax.axis_index("fsdp") % 2
    groups = [list(range(c, shards, 2)) for c in range(2)]
    micro, local, width = inputs.shape
    gain_row = gain[0]
    gate_w, up_w, down_w = w_gate[0], w_up[0], w_down[0]
    experts = gate_w.shape[0]
    coef = combine_weights(routes[0], shares[0], experts, shards)
    coef = coef.reshape(experts, chips, 2, micro * local)
    coef_mine = lax.dynamic_index_in_dim(coef, core, 2, keepdims=False)
    coef_other = lax.dynamic_index_in_dim(coef, 1 - core, 2, keepdims=False)
    current = inputs.reshape(micro * local, width)
    output = jnp.zeros_like(current)
    for tick in range(sections):
        if tick > 0:
            current = passed_along(result, "section", 1)
        normed = rms_norm(current, gain_row)
        spread = jnp.broadcast_to(normed[None], (chips,) + normed.shape)
        near = lax.all_to_all(spread, "fsdp", 0, 0, tiled=True, axis_index_groups=groups)
        far = sibling(near, "fsdp")
        part_near = expert_mix(near, coef_mine, gate_w, up_w, down_w)
        part_far = expert_mix(far, coef_other, gate_w, up_w, down_w)
        chip_sum = part_near + sibling(part_far, "fsdp")
        pieces = lax.all_to_all(
            chip_sum.astype(jnp.bfloat16), "fsdp", 0, 0, tiled=True, axis_index_groups=groups
        )
        mixed = jnp.sum(pieces.astype(jnp.float32), axis=0)
        result = (current.astype(jnp.float32) + mixed).astype(jnp.bfloat16)
        output = jnp.where(section_index == tick, result, output)
    return output.reshape(1, micro, local, width)


def solution(mesh):
    placed = (
        P(None, "fsdp", None),
        P("section", None),
        P("section", None, None, "fsdp"),
        P("section", None, None, "fsdp"),
        P("section", None, "fsdp", None),
        P("section", None, None, None),
        P("section", None, None, None),
    )
    return jax.shard_map(
        on_device,
        mesh=mesh,
        in_specs=placed,
        out_specs=P("section", None, "fsdp", None),
        check_vma=False,
    )
```

```python
import jax
import jax.numpy as jnp
from jax import lax
from jax.sharding import PartitionSpec as P


def passed_along(array, axis, by):
    devices = lax.axis_size(axis)
    pairs = [(i, i + by) for i in range(devices) if 0 <= i + by < devices]
    return lax.ppermute(array, axis, pairs)


def sibling(array, axis):
    devices = lax.axis_size(axis)
    return lax.ppermute(array, axis, [(i, i ^ 1) for i in range(devices)])


def torus_shifts(side):
    return [(dx, dz) for dx in range(side) for dz in range(side)]


def shifted(array, axis, side, dx, dz):
    devices = lax.axis_size(axis)
    pairs = []
    for f in range(devices):
        chip, core = divmod(f, 2)
        x, z = divmod(chip, side)
        target = (((x + dx) % side) * side + (z + dz) % side) * 2 + core
        pairs.append((f, target))
    return lax.ppermute(array, axis, pairs)


def rms_norm(rows, gain_row):
    values = rows.astype(jnp.float32)
    scale = lax.rsqrt(jnp.mean(values * values, axis=-1, keepdims=True) + 1e-05)
    return (values * scale * gain_row[None, :]).astype(jnp.bfloat16)


def combine_weights(route_layer, share_layer, experts, shards):
    micro, tokens, top = route_layer.shape
    per = tokens // shards
    onehot = (route_layer[..., None] == jnp.arange(experts, dtype=route_layer.dtype)).astype(jnp.float32)
    coef = jnp.sum(onehot * share_layer[..., None], axis=2)
    coef = coef.reshape(micro, shards, per, experts).transpose(3, 1, 0, 2)
    return coef.reshape(experts, shards, micro * per)


def expert_mix(rows, coef, gate_w, up_w, down_w):
    gate = jnp.einsum("fmd,edh->efmh", rows, gate_w, preferred_element_type=jnp.float32)
    upward = jnp.einsum("fmd,edh->efmh", rows, up_w, preferred_element_type=jnp.float32)
    gated = (jax.nn.silu(gate) * upward * coef[..., None]).astype(jnp.bfloat16)
    return jnp.einsum("efmh,ehd->fmd", gated, down_w, preferred_element_type=jnp.float32)


def on_device(inputs, gain, w_gate, w_up, w_down, routes, shares):
    sections = lax.axis_size("section")
    shards = lax.axis_size("fsdp")
    chips = shards // 2
    section_index = lax.axis_index("section")
    me = lax.axis_index("fsdp")
    core = me % 2
    side = int(round(chips ** 0.5))
    shifts = torus_shifts(side)
    my_x, my_z = (me // 2) // side, (me // 2) % side
    micro, local, width = inputs.shape
    gain_row = gain[0]
    gate_w, up_w, down_w = w_gate[0], w_up[0], w_down[0]
    experts = gate_w.shape[0]
    coef = combine_weights(routes[0], shares[0], experts, shards)
    source_chip = jnp.stack(
        [((my_x - dx) % side) * side + (my_z - dz) % side for dx, dz in shifts]
    )
    coef_mine = jnp.take(coef, source_chip * 2 + core, axis=1)
    coef_other = jnp.take(coef, source_chip * 2 + 1 - core, axis=1)
    back = [shifts.index(((side - dx) % side, (side - dz) % side)) for dx, dz in shifts]
    current = inputs.reshape(micro * local, width)
    output = jnp.zeros_like(current)
    for tick in range(sections):
        if tick > 0:
            current = passed_along(result, "section", 1)
        normed = rms_norm(current, gain_row)
        near = jnp.stack(
            [normed if (dx, dz) == (0, 0) else shifted(normed, "fsdp", side, dx, dz) for dx, dz in shifts]
        )
        far = sibling(near, "fsdp")
        part_near = expert_mix(near, coef_mine, gate_w, up_w, down_w)
        part_far = expert_mix(far, coef_other, gate_w, up_w, down_w)
        chip_sum = part_near + sibling(part_far, "fsdp")
        sent = chip_sum.astype(jnp.bfloat16)
        mixed = chip_sum[back[0]]
        for (dx, dz), k in zip(shifts[1:], back[1:]):
            mixed = mixed + shifted(sent[k], "fsdp", side, dx, dz).astype(jnp.float32)
        result = (current.astype(jnp.float32) + mixed).astype(jnp.bfloat16)
        output = jnp.where(section_index == tick, result, output)
    return output.reshape(1, micro, local, width)


def solution(mesh):
    placed = (
        P(None, "fsdp", None),
        P("section", None),
        P("section", None, None, "fsdp"),
        P("section", None, None, "fsdp"),
        P("section", None, "fsdp", None),
        P("section", None, None, None),
        P("section", None, None, None),
    )
    return jax.shard_map(
        on_device,
        mesh=mesh,
        in_specs=placed,
        out_specs=P("section", None, "fsdp", None),
        check_vma=False,
    )
```

```python
import jax
import jax.numpy as jnp
from jax import lax
from jax.experimental import pallas as pl
from jax.experimental.pallas import tpu as pltpu
from jax.sharding import PartitionSpec as P

MESH = pl.DeviceIdType.MESH


def exchange(src, chips, same, collective_id):
    rows, width = src.shape[-2:]

    def kernel(src_ref, out_ref, send_sem, recv_sem, local_sem):
        me = lax.axis_index("fsdp")
        section = lax.axis_index("section")
        chip, core = me // 2, me % 2
        barrier = pltpu.get_barrier_semaphore()
        for j in range(1, chips):
            peer = lax.rem(chip + j, chips)
            pl.semaphore_signal(barrier, 1, device_id=(section, peer * 2 + core), device_id_type=MESH)
        pl.semaphore_wait(barrier, chips - 1)
        local = pltpu.make_async_copy(src_ref if same else src_ref.at[chip], out_ref.at[chip], local_sem)
        local.start()
        copies = []
        for j in range(1, chips):
            peer = lax.rem(chip + j, chips)
            copy = pltpu.make_async_remote_copy(
                src_ref=src_ref if same else src_ref.at[peer],
                dst_ref=out_ref.at[chip],
                send_sem=send_sem.at[j],
                recv_sem=recv_sem.at[j],
                device_id=(section, peer * 2 + core),
                device_id_type=MESH,
            )
            copy.start()
            copies.append(copy)
        local.wait()
        for copy in copies:
            copy.wait()

    return pl.pallas_call(
        kernel,
        out_shape=jax.ShapeDtypeStruct((chips, rows, width), src.dtype),
        in_specs=[pl.BlockSpec(memory_space=pl.ANY)],
        out_specs=pl.BlockSpec(memory_space=pl.ANY),
        scratch_shapes=[
            pltpu.SemaphoreType.DMA((chips,)),
            pltpu.SemaphoreType.DMA((chips,)),
            pltpu.SemaphoreType.DMA(()),
        ],
        compiler_params=pltpu.CompilerParams(collective_id=collective_id, has_side_effects=True),
    )(src)


def passed_along(array, axis, by):
    devices = lax.axis_size(axis)
    pairs = [(i, i + by) for i in range(devices) if 0 <= i + by < devices]
    return lax.ppermute(array, axis, pairs)


def sibling(array, axis):
    devices = lax.axis_size(axis)
    return lax.ppermute(array, axis, [(i, i ^ 1) for i in range(devices)])


def rms_norm(rows, gain_row):
    values = rows.astype(jnp.float32)
    scale = lax.rsqrt(jnp.mean(values * values, axis=-1, keepdims=True) + 1e-05)
    return (values * scale * gain_row[None, :]).astype(jnp.bfloat16)


def combine_weights(route_layer, share_layer, experts, shards):
    micro, tokens, top = route_layer.shape
    per = tokens // shards
    onehot = (route_layer[..., None] == jnp.arange(experts, dtype=route_layer.dtype)).astype(jnp.float32)
    coef = jnp.sum(onehot * share_layer[..., None], axis=2)
    coef = coef.reshape(micro, shards, per, experts).transpose(3, 1, 0, 2)
    return coef.reshape(experts, shards, micro * per)


def expert_mix(rows, coef, gate_w, up_w, down_w):
    gate = jnp.einsum("fmd,edh->efmh", rows, gate_w, preferred_element_type=jnp.float32)
    upward = jnp.einsum("fmd,edh->efmh", rows, up_w, preferred_element_type=jnp.float32)
    gated = (jax.nn.silu(gate) * upward * coef[..., None]).astype(jnp.bfloat16)
    return jnp.einsum("efmh,ehd->fmd", gated, down_w, preferred_element_type=jnp.float32)


def on_device(inputs, gain, w_gate, w_up, w_down, routes, shares):
    sections = lax.axis_size("section")
    shards = lax.axis_size("fsdp")
    chips = shards // 2
    section_index = lax.axis_index("section")
    core = lax.axis_index("fsdp") % 2
    micro, local, width = inputs.shape
    gain_row = gain[0]
    gate_w, up_w, down_w = w_gate[0], w_up[0], w_down[0]
    experts = gate_w.shape[0]
    coef = combine_weights(routes[0], shares[0], experts, shards)
    coef = coef.reshape(experts, chips, 2, micro * local)
    coef_mine = lax.dynamic_index_in_dim(coef, core, 2, keepdims=False)
    coef_other = lax.dynamic_index_in_dim(coef, 1 - core, 2, keepdims=False)
    current = inputs.reshape(micro * local, width)
    output = jnp.zeros_like(current)
    for tick in range(sections):
        if tick > 0:
            current = passed_along(result, "section", 1)
        normed = rms_norm(current, gain_row)
        near = exchange(normed, chips, True, 0)
        far = sibling(near, "fsdp")
        part_near = expert_mix(near, coef_mine, gate_w, up_w, down_w)
        part_far = expert_mix(far, coef_other, gate_w, up_w, down_w)
        chip_sum = part_near + sibling(part_far, "fsdp")
        pieces = exchange(chip_sum.astype(jnp.bfloat16), chips, False, 1)
        mixed = jnp.sum(pieces.astype(jnp.float32), axis=0)
        result = (current.astype(jnp.float32) + mixed).astype(jnp.bfloat16)
        output = jnp.where(section_index == tick, result, output)
    return output.reshape(1, micro, local, width)


def solution(mesh):
    placed = (
        P(None, "fsdp", None),
        P("section", None),
        P("section", None, None, "fsdp"),
        P("section", None, None, "fsdp"),
        P("section", None, "fsdp", None),
        P("section", None, None, None),
        P("section", None, None, None),
    )
    return jax.shard_map(
        on_device,
        mesh=mesh,
        in_specs=placed,
        out_specs=P("section", None, "fsdp", None),
        check_vma=False,
    )
```

```python
import jax
import jax.numpy as jnp
from jax import lax
from jax.sharding import PartitionSpec as P


def passed_along(array, axis, by):
    devices = lax.axis_size(axis)
    pairs = [(i, i + by) for i in range(devices) if 0 <= i + by < devices]
    return lax.ppermute(array, axis, pairs)


def sibling(array, axis):
    devices = lax.axis_size(axis)
    return lax.ppermute(array, axis, [(i, i ^ 1) for i in range(devices)])


def rms_norm(rows, gain_row):
    values = rows.astype(jnp.float32)
    scale = lax.rsqrt(jnp.mean(values * values, axis=-1, keepdims=True) + 1e-05)
    return (values * scale * gain_row[None, :]).astype(jnp.bfloat16)


def combine_weights(route_layer, share_layer, experts, shards):
    micro, tokens, top = route_layer.shape
    per = tokens // shards
    onehot = (route_layer[..., None] == jnp.arange(experts, dtype=route_layer.dtype)).astype(jnp.float32)
    coef = jnp.sum(onehot * share_layer[..., None], axis=2)
    return coef.reshape(micro, shards, per, experts).transpose(0, 3, 1, 2)


def expert_mix(rows, coef, gate_w, up_w, down_w):
    gate = jnp.einsum("fmd,edh->efmh", rows, gate_w, preferred_element_type=jnp.float32)
    upward = jnp.einsum("fmd,edh->efmh", rows, up_w, preferred_element_type=jnp.float32)
    gated = (jax.nn.silu(gate) * upward * coef[..., None]).astype(jnp.bfloat16)
    return jnp.einsum("efmh,ehd->fmd", gated, down_w, preferred_element_type=jnp.float32)


def on_device(inputs, gain, w_gate, w_up, w_down, routes, shares):
    sections = lax.axis_size("section")
    shards = lax.axis_size("fsdp")
    chips = shards // 2
    section_index = lax.axis_index("section")
    core = lax.axis_index("fsdp") % 2
    groups = [list(range(c, shards, 2)) for c in range(2)]
    micro, local, width = inputs.shape
    gain_row = gain[0]
    gate_w, up_w, down_w = w_gate[0], w_up[0], w_down[0]
    experts = gate_w.shape[0]
    coef = combine_weights(routes[0], shares[0], experts, shards)
    coef = coef.reshape(micro, experts, chips, 2, local)
    coef = jnp.concatenate(
        [
            lax.dynamic_index_in_dim(coef, core, 3, keepdims=False),
            lax.dynamic_index_in_dim(coef, 1 - core, 3, keepdims=False),
        ],
        axis=2,
    )
    output = jnp.zeros_like(inputs)
    carried = None
    for tick in range(micro + sections - 1):
        position = tick - section_index
        valid = jnp.logical_and(position >= 0, position < micro)
        clipped = jnp.clip(position, 0, micro - 1)
        entry = lax.dynamic_index_in_dim(inputs, clipped, 0, keepdims=False)
        coef_now = lax.dynamic_index_in_dim(coef, clipped, 0, keepdims=False)
        current = entry if carried is None else jnp.where(section_index == 0, entry, carried)
        normed = rms_norm(current, gain_row)
        spread = jnp.broadcast_to(normed[None], (chips,) + normed.shape)
        near = lax.all_to_all(spread, "fsdp", 0, 0, tiled=True, axis_index_groups=groups)
        rows = jnp.concatenate([near, sibling(near, "fsdp")], axis=0)
        partial_value = expert_mix(rows, coef_now, gate_w, up_w, down_w)
        chip_sum = partial_value[:chips] + sibling(partial_value[chips:], "fsdp")
        pieces = lax.all_to_all(
            chip_sum.astype(jnp.bfloat16), "fsdp", 0, 0, tiled=True, axis_index_groups=groups
        )
        mixed = jnp.sum(pieces.astype(jnp.float32), axis=0)
        result = (current.astype(jnp.float32) + mixed).astype(jnp.bfloat16)
        if tick + 1 < micro + sections - 1:
            carried = passed_along(result, "section", 1)
        updated = lax.dynamic_update_index_in_dim(output, result, clipped, 0)
        output = jnp.where(valid, updated, output)
    return output[None]


def solution(mesh):
    placed = (
        P(None, "fsdp", None),
        P("section", None),
        P("section", None, None, "fsdp"),
        P("section", None, None, "fsdp"),
        P("section", None, "fsdp", None),
        P("section", None, None, None),
        P("section", None, None, None),
    )
    return jax.shard_map(
        on_device,
        mesh=mesh,
        in_specs=placed,
        out_specs=P("section", None, "fsdp", None),
        check_vma=False,
    )
```

```python
import jax
import jax.numpy as jnp
from jax import lax
from jax.experimental import pallas as pl
from jax.experimental.pallas import tpu as pltpu
from jax.sharding import PartitionSpec as P

MESH = pl.DeviceIdType.MESH


def exchange(src, shards, same, collective_id):
    rows, width = src.shape[-2:]

    def kernel(src_ref, out_ref, send_sem, recv_sem, local_sem):
        me = lax.axis_index("fsdp")
        section = lax.axis_index("section")
        barrier = pltpu.get_barrier_semaphore()
        for j in range(1, shards):
            peer = lax.rem(me + j, shards)
            pl.semaphore_signal(barrier, 1, device_id=(section, peer), device_id_type=MESH)
        pl.semaphore_wait(barrier, shards - 1)
        local = pltpu.make_async_copy(src_ref if same else src_ref.at[me], out_ref.at[me], local_sem)
        local.start()
        copies = []
        for j in range(1, shards):
            peer = lax.rem(me + j, shards)
            copy = pltpu.make_async_remote_copy(
                src_ref=src_ref if same else src_ref.at[peer],
                dst_ref=out_ref.at[me],
                send_sem=send_sem.at[j],
                recv_sem=recv_sem.at[j],
                device_id=(section, peer),
                device_id_type=MESH,
            )
            copy.start()
            copies.append(copy)
        local.wait()
        for copy in copies:
            copy.wait()

    return pl.pallas_call(
        kernel,
        out_shape=jax.ShapeDtypeStruct((shards, rows, width), src.dtype),
        in_specs=[pl.BlockSpec(memory_space=pl.ANY)],
        out_specs=pl.BlockSpec(memory_space=pl.ANY),
        scratch_shapes=[
            pltpu.SemaphoreType.DMA((shards,)),
            pltpu.SemaphoreType.DMA((shards,)),
            pltpu.SemaphoreType.DMA(()),
        ],
        compiler_params=pltpu.CompilerParams(collective_id=collective_id, has_side_effects=True),
    )(src)


def passed_along(array, axis, by):
    devices = lax.axis_size(axis)
    pairs = [(i, i + by) for i in range(devices) if 0 <= i + by < devices]
    return lax.ppermute(array, axis, pairs)


def sibling(array, axis):
    devices = lax.axis_size(axis)
    return lax.ppermute(array, axis, [(i, i ^ 1) for i in range(devices)])


def rms_norm(rows, gain_row):
    values = rows.astype(jnp.float32)
    scale = lax.rsqrt(jnp.mean(values * values, axis=-1, keepdims=True) + 1e-05)
    return (values * scale * gain_row[None, :]).astype(jnp.bfloat16)


def combine_weights(route_layer, share_layer, experts, shards):
    micro, tokens, top = route_layer.shape
    per = tokens // shards
    onehot = (route_layer[..., None] == jnp.arange(experts, dtype=route_layer.dtype)).astype(jnp.float32)
    coef = jnp.sum(onehot * share_layer[..., None], axis=2)
    return coef.reshape(micro, shards, per, experts).transpose(0, 3, 1, 2)


def expert_mix(rows, coef, gate_w, up_w, down_w):
    gate = jnp.einsum("fmd,edh->efmh", rows, gate_w, preferred_element_type=jnp.float32)
    upward = jnp.einsum("fmd,edh->efmh", rows, up_w, preferred_element_type=jnp.float32)
    gated = (jax.nn.silu(gate) * upward * coef[..., None]).astype(jnp.bfloat16)
    return jnp.einsum("efmh,ehd->fmd", gated, down_w, preferred_element_type=jnp.float32)


def on_device(inputs, gain, w_gate, w_up, w_down, routes, shares):
    sections = lax.axis_size("section")
    shards = lax.axis_size("fsdp")
    chips = shards // 2
    section_index = lax.axis_index("section")
    micro, local, width = inputs.shape
    gain_row = gain[0]
    gate_w, up_w, down_w = w_gate[0], w_up[0], w_down[0]
    experts = gate_w.shape[0]
    coef = combine_weights(routes[0], shares[0], experts, shards)
    output = jnp.zeros_like(inputs)
    carried = None
    for tick in range(micro + sections - 1):
        position = tick - section_index
        valid = jnp.logical_and(position >= 0, position < micro)
        clipped = jnp.clip(position, 0, micro - 1)
        entry = lax.dynamic_index_in_dim(inputs, clipped, 0, keepdims=False)
        coef_now = lax.dynamic_index_in_dim(coef, clipped, 0, keepdims=False)
        current = entry if carried is None else jnp.where(section_index == 0, entry, carried)
        normed = rms_norm(current, gain_row)
        lanes = local * width // 128
        rows = exchange(normed.reshape(lanes, 128), shards, True, 0).reshape(shards, local, width)
        partial_value = expert_mix(rows, coef_now, gate_w, up_w, down_w)
        sent = partial_value.astype(jnp.bfloat16).reshape(shards, lanes, 128)
        pieces = exchange(sent, shards, False, 1)
        mixed = jnp.sum(pieces.astype(jnp.float32), axis=0).reshape(local, width)
        result = (current.astype(jnp.float32) + mixed).astype(jnp.bfloat16)
        if tick + 1 < micro + sections - 1:
            carried = passed_along(result, "section", 1)
        updated = lax.dynamic_update_index_in_dim(output, result, clipped, 0)
        output = jnp.where(valid, updated, output)
    return output[None]


def solution(mesh):
    placed = (
        P(None, "fsdp", None),
        P("section", None),
        P("section", None, None, "fsdp"),
        P("section", None, None, "fsdp"),
        P("section", None, "fsdp", None),
        P("section", None, None, None),
        P("section", None, None, None),
    )
    return jax.shard_map(
        on_device,
        mesh=mesh,
        in_specs=placed,
        out_specs=P("section", None, "fsdp", None),
        check_vma=False,
    )
```

```python
import jax
import jax.numpy as jnp
from jax import lax
from jax.sharding import PartitionSpec as P
from jax.experimental import pallas as pl
from jax.experimental.pallas import tpu as pltpu

MESH = pl.DeviceIdType.MESH


def exchange(src, chips, same, collective_id):
    rows, width = src.shape[-2:]

    def kernel(src_ref, out_ref, send_sem, recv_sem, local_sem):
        me = lax.axis_index("fsdp")
        section = lax.axis_index("section")
        chip, core = me // 2, me % 2
        barrier = pltpu.get_barrier_semaphore()
        for j in range(1, chips):
            peer = lax.rem(chip + j, chips)
            pl.semaphore_signal(barrier, 1, device_id=(section, peer * 2 + core), device_id_type=MESH)
        pl.semaphore_wait(barrier, chips - 1)
        local = pltpu.make_async_copy(src_ref if same else src_ref.at[chip], out_ref.at[chip], local_sem)
        local.start()
        copies = []
        for j in range(1, chips):
            peer = lax.rem(chip + j, chips)
            copy = pltpu.make_async_remote_copy(
                src_ref=src_ref if same else src_ref.at[peer],
                dst_ref=out_ref.at[chip],
                send_sem=send_sem.at[j],
                recv_sem=recv_sem.at[j],
                device_id=(section, peer * 2 + core),
                device_id_type=MESH,
            )
            copy.start()
            copies.append(copy)
        local.wait()
        for copy in copies:
            copy.wait()

    return pl.pallas_call(
        kernel,
        out_shape=jax.ShapeDtypeStruct((chips, rows, width), src.dtype),
        in_specs=[pl.BlockSpec(memory_space=pl.ANY)],
        out_specs=pl.BlockSpec(memory_space=pl.ANY),
        scratch_shapes=[
            pltpu.SemaphoreType.DMA((chips,)),
            pltpu.SemaphoreType.DMA((chips,)),
            pltpu.SemaphoreType.DMA(()),
        ],
        compiler_params=pltpu.CompilerParams(collective_id=collective_id, has_side_effects=True),
    )(src)


def passed_along(array, axis, by):
    devices = lax.axis_size(axis)
    pairs = [(i, i + by) for i in range(devices) if 0 <= i + by < devices]
    return lax.ppermute(array, axis, pairs)


def sibling(array, axis):
    devices = lax.axis_size(axis)
    return lax.ppermute(array, axis, [(i, i ^ 1) for i in range(devices)])


def rms_norm(rows, gain_row):
    values = rows.astype(jnp.float32)
    scale = lax.rsqrt(jnp.mean(values * values, axis=-1, keepdims=True) + 1e-05)
    return (values * scale * gain_row[None, :]).astype(jnp.bfloat16)


def combine_weights(route_layer, share_layer, experts, shards):
    micro, tokens, top = route_layer.shape
    per = tokens // shards
    onehot = (route_layer[..., None] == jnp.arange(experts, dtype=route_layer.dtype)).astype(jnp.float32)
    coef = jnp.sum(onehot * share_layer[..., None], axis=2)
    return coef.reshape(micro, shards, per, experts).transpose(0, 3, 1, 2)


def expert_mix(rows, coef, gate_w, up_w, down_w):
    gate = jnp.einsum("fmd,edh->efmh", rows, gate_w, preferred_element_type=jnp.float32)
    upward = jnp.einsum("fmd,edh->efmh", rows, up_w, preferred_element_type=jnp.float32)
    gated = (jax.nn.silu(gate) * upward * coef[..., None]).astype(jnp.bfloat16)
    return jnp.einsum("efmh,ehd->fmd", gated, down_w, preferred_element_type=jnp.float32)


def on_device(inputs, gain, w_gate, w_up, w_down, routes, shares):
    sections = lax.axis_size("section")
    shards = lax.axis_size("fsdp")
    chips = shards // 2
    section_index = lax.axis_index("section")
    core = lax.axis_index("fsdp") % 2
    micro, local, width = inputs.shape
    gain_row = gain[0]
    gate_w, up_w, down_w = w_gate[0], w_up[0], w_down[0]
    experts = gate_w.shape[0]
    coef = combine_weights(routes[0], shares[0], experts, shards)
    coef = coef.reshape(micro, experts, chips, 2, local)
    coef = jnp.concatenate(
        [
            lax.dynamic_index_in_dim(coef, core, 3, keepdims=False),
            lax.dynamic_index_in_dim(coef, 1 - core, 3, keepdims=False),
        ],
        axis=2,
    )
    output = jnp.zeros_like(inputs)
    carried = None
    for tick in range(micro + sections - 1):
        position = tick - section_index
        valid = jnp.logical_and(position >= 0, position < micro)
        clipped = jnp.clip(position, 0, micro - 1)
        entry = lax.dynamic_index_in_dim(inputs, clipped, 0, keepdims=False)
        coef_now = lax.dynamic_index_in_dim(coef, clipped, 0, keepdims=False)
        current = entry if carried is None else jnp.where(section_index == 0, entry, carried)
        normed = rms_norm(current, gain_row)
        lanes = local * width // 128
        near = exchange(normed.reshape(lanes, 128), chips, True, 0)
        rows = jnp.concatenate([near, sibling(near, "fsdp")], axis=0).reshape(shards, local, width)
        partial_value = expert_mix(rows, coef_now, gate_w, up_w, down_w)
        chip_sum = partial_value[:chips] + sibling(partial_value[chips:], "fsdp")
        sent = chip_sum.astype(jnp.bfloat16).reshape(chips, lanes, 128)
        pieces = exchange(sent, chips, False, 1)
        mixed = jnp.sum(pieces.astype(jnp.float32), axis=0).reshape(local, width)
        result = (current.astype(jnp.float32) + mixed).astype(jnp.bfloat16)
        if tick + 1 < micro + sections - 1:
            carried = passed_along(result, "section", 1)
        updated = lax.dynamic_update_index_in_dim(output, result, clipped, 0)
        output = jnp.where(valid, updated, output)
    return output[None]


def solution(mesh):
    placed = (
        P(None, "fsdp", None),
        P("section", None),
        P("section", None, None, "fsdp"),
        P("section", None, None, "fsdp"),
        P("section", None, "fsdp", None),
        P("section", None, None, None),
        P("section", None, None, None),
    )
    return jax.shard_map(
        on_device,
        mesh=mesh,
        in_specs=placed,
        out_specs=P("section", None, "fsdp", None),
        check_vma=False,
    )
```

```python
import jax
import jax.numpy as jnp
from jax import lax
from jax.sharding import PartitionSpec as P
from jax.experimental import pallas as pl
from jax.experimental.pallas import tpu as pltpu

MESH = pl.DeviceIdType.MESH


def exchange(src, chips, same, collective_id):
    rows, width = src.shape[-2:]

    def kernel(src_ref, out_ref, send_sem, recv_sem, local_sem):
        me = lax.axis_index("fsdp")
        section = lax.axis_index("section")
        chip, core = me // 2, me % 2
        barrier = pltpu.get_barrier_semaphore()
        for j in range(1, chips):
            peer = lax.rem(chip + j, chips)
            pl.semaphore_signal(barrier, 1, device_id=(section, peer * 2 + core), device_id_type=MESH)
        pl.semaphore_wait(barrier, chips - 1)
        local = pltpu.make_async_copy(src_ref if same else src_ref.at[chip], out_ref.at[chip], local_sem)
        local.start()
        copies = []
        for j in range(1, chips):
            peer = lax.rem(chip + j, chips)
            copy = pltpu.make_async_remote_copy(
                src_ref=src_ref if same else src_ref.at[peer],
                dst_ref=out_ref.at[chip],
                send_sem=send_sem.at[j],
                recv_sem=recv_sem.at[j],
                device_id=(section, peer * 2 + core),
                device_id_type=MESH,
            )
            copy.start()
            copies.append(copy)
        local.wait()
        for copy in copies:
            copy.wait()

    return pl.pallas_call(
        kernel,
        out_shape=jax.ShapeDtypeStruct((chips, rows, width), src.dtype),
        in_specs=[pl.BlockSpec(memory_space=pl.ANY)],
        out_specs=pl.BlockSpec(memory_space=pl.ANY),
        scratch_shapes=[
            pltpu.SemaphoreType.DMA((chips,)),
            pltpu.SemaphoreType.DMA((chips,)),
            pltpu.SemaphoreType.DMA(()),
        ],
        compiler_params=pltpu.CompilerParams(collective_id=collective_id, has_side_effects=True),
    )(src)


def passed_along(array, axis, by):
    devices = lax.axis_size(axis)
    pairs = [(i, i + by) for i in range(devices) if 0 <= i + by < devices]
    return lax.ppermute(array, axis, pairs)


def sibling(array, axis):
    devices = lax.axis_size(axis)
    return lax.ppermute(array, axis, [(i, i ^ 1) for i in range(devices)])


def rms_norm(rows, gain_row):
    values = rows.astype(jnp.float32)
    scale = lax.rsqrt(jnp.mean(values * values, axis=-1, keepdims=True) + 1e-05)
    return (values * scale * gain_row[None, :]).astype(jnp.bfloat16)


def combine_weights(route_layer, share_layer, experts, shards):
    micro, tokens, top = route_layer.shape
    per = tokens // shards
    onehot = (route_layer[..., None] == jnp.arange(experts, dtype=route_layer.dtype)).astype(jnp.float32)
    coef = jnp.sum(onehot * share_layer[..., None], axis=2)
    return coef.reshape(micro, shards, per, experts).transpose(0, 3, 1, 2)


def expert_mix(rows, coef, gate_w, up_w, down_w):
    tokens = rows.shape[0]
    experts = coef.shape[1]
    hidden = gate_w.shape[1] // experts
    gate = jnp.dot(rows, gate_w, preferred_element_type=jnp.float32)
    upward = jnp.dot(rows, up_w, preferred_element_type=jnp.float32)
    spread = jnp.broadcast_to(coef[:, :, None], (tokens, experts, hidden)).reshape(tokens, experts * hidden)
    gated = (jax.nn.silu(gate) * upward * spread).astype(jnp.bfloat16)
    return jnp.dot(gated, down_w, preferred_element_type=jnp.float32)


def on_device(inputs, gain, w_gate, w_up, w_down, routes, shares):
    sections = lax.axis_size("section")
    shards = lax.axis_size("fsdp")
    chips = shards // 2
    section_index = lax.axis_index("section")
    core = lax.axis_index("fsdp") % 2
    micro, local, width = inputs.shape
    gain_row = gain[0]
    experts, _, hidden = w_gate.shape[1:]
    gate_w = w_gate[0].transpose(1, 0, 2).reshape(width, experts * hidden)
    up_w = w_up[0].transpose(1, 0, 2).reshape(width, experts * hidden)
    down_w = w_down[0].reshape(experts * hidden, width)
    coef = combine_weights(routes[0], shares[0], experts, shards)
    coef = coef.reshape(micro, experts, chips, 2, local)
    coef = jnp.concatenate(
        [
            lax.dynamic_index_in_dim(coef, core, 3, keepdims=False),
            lax.dynamic_index_in_dim(coef, 1 - core, 3, keepdims=False),
        ],
        axis=2,
    )
    coef = coef.transpose(0, 2, 3, 1).reshape(micro, shards * local, experts)
    output = jnp.zeros_like(inputs)
    carried = None
    for tick in range(micro + sections - 1):
        position = tick - section_index
        valid = jnp.logical_and(position >= 0, position < micro)
        clipped = jnp.clip(position, 0, micro - 1)
        entry = lax.dynamic_index_in_dim(inputs, clipped, 0, keepdims=False)
        coef_now = lax.dynamic_index_in_dim(coef, clipped, 0, keepdims=False)
        current = entry if carried is None else jnp.where(section_index == 0, entry, carried)
        normed = rms_norm(current, gain_row)
        lanes = local * width // 128
        near = exchange(normed.reshape(lanes, 128), chips, True, 0)
        rows = jnp.concatenate([near, sibling(near, "fsdp")], axis=0).reshape(shards * local, width)
        partial_value = expert_mix(rows, coef_now, gate_w, up_w, down_w).reshape(shards, local, width)
        chip_sum = partial_value[:chips] + sibling(partial_value[chips:], "fsdp")
        sent = chip_sum.astype(jnp.bfloat16).reshape(chips, lanes, 128)
        pieces = exchange(sent, chips, False, 1)
        mixed = jnp.sum(pieces.astype(jnp.float32), axis=0).reshape(local, width)
        result = (current.astype(jnp.float32) + mixed).astype(jnp.bfloat16)
        if tick + 1 < micro + sections - 1:
            carried = passed_along(result, "section", 1)
        updated = lax.dynamic_update_index_in_dim(output, result, clipped, 0)
        output = jnp.where(valid, updated, output)
    return output[None]


def solution(mesh):
    placed = (
        P(None, "fsdp", None),
        P("section", None),
        P("section", None, None, "fsdp"),
        P("section", None, None, "fsdp"),
        P("section", None, "fsdp", None),
        P("section", None, None, None),
        P("section", None, None, None),
    )
    return jax.shard_map(
        on_device,
        mesh=mesh,
        in_specs=placed,
        out_specs=P("section", None, "fsdp", None),
        check_vma=False,
    )
```

```python
import jax
import jax.numpy as jnp
from jax import lax
from jax.sharding import PartitionSpec as P
from jax.experimental import pallas as pl
from jax.experimental.pallas import tpu as pltpu

MESH = pl.DeviceIdType.MESH


def exchange(src, chips, same, collective_id):
    rows, width = src.shape[-2:]

    def kernel(src_ref, out_ref, send_sem, recv_sem, local_sem):
        me = lax.axis_index("fsdp")
        section = lax.axis_index("section")
        chip, core = me // 2, me % 2
        barrier = pltpu.get_barrier_semaphore()
        for j in range(1, chips):
            peer = lax.rem(chip + j, chips)
            pl.semaphore_signal(barrier, 1, device_id=(section, peer * 2 + core), device_id_type=MESH)
        pl.semaphore_wait(barrier, chips - 1)
        local = pltpu.make_async_copy(src_ref if same else src_ref.at[chip], out_ref.at[chip], local_sem)
        local.start()
        copies = []
        for j in range(1, chips):
            peer = lax.rem(chip + j, chips)
            copy = pltpu.make_async_remote_copy(
                src_ref=src_ref if same else src_ref.at[peer],
                dst_ref=out_ref.at[chip],
                send_sem=send_sem.at[j],
                recv_sem=recv_sem.at[j],
                device_id=(section, peer * 2 + core),
                device_id_type=MESH,
            )
            copy.start()
            copies.append(copy)
        local.wait()
        for copy in copies:
            copy.wait()

    return pl.pallas_call(
        kernel,
        out_shape=jax.ShapeDtypeStruct((chips, rows, width), src.dtype),
        in_specs=[pl.BlockSpec(memory_space=pl.ANY)],
        out_specs=pl.BlockSpec(memory_space=pl.ANY),
        scratch_shapes=[
            pltpu.SemaphoreType.DMA((chips,)),
            pltpu.SemaphoreType.DMA((chips,)),
            pltpu.SemaphoreType.DMA(()),
        ],
        compiler_params=pltpu.CompilerParams(collective_id=collective_id, has_side_effects=True),
    )(src)


def passed_along(array, axis, by):
    devices = lax.axis_size(axis)
    pairs = [(i, i + by) for i in range(devices) if 0 <= i + by < devices]
    return lax.ppermute(array, axis, pairs)


def sibling(array, axis):
    devices = lax.axis_size(axis)
    return lax.ppermute(array, axis, [(i, i ^ 1) for i in range(devices)])


def rms_norm(rows, gain_row):
    values = rows.astype(jnp.float32)
    scale = lax.rsqrt(jnp.mean(values * values, axis=-1, keepdims=True) + 1e-05)
    return (values * scale * gain_row[None, :]).astype(jnp.bfloat16)


def combine_weights(route_layer, share_layer, experts, shards):
    micro, tokens, top = route_layer.shape
    per = tokens // shards
    onehot = (route_layer[..., None] == jnp.arange(experts, dtype=route_layer.dtype)).astype(jnp.float32)
    coef = jnp.sum(onehot * share_layer[..., None], axis=2)
    return coef.reshape(micro, shards, per, experts).transpose(0, 3, 1, 2)


def expert_kernel(rows_ref, coef_ref, gate_ref, up_ref, down_ref, out_ref):
    expert = pl.program_id(0)

    @pl.when(expert == 0)
    def _():
        out_ref[...] = jnp.zeros_like(out_ref)

    rows = rows_ref[...]
    gate = jnp.dot(rows, gate_ref[0], preferred_element_type=jnp.float32)
    upward = jnp.dot(rows, up_ref[0], preferred_element_type=jnp.float32)
    gated = (jax.nn.silu(gate) * upward * coef_ref[0]).astype(jnp.bfloat16)
    out_ref[...] += jnp.dot(gated, down_ref[0], preferred_element_type=jnp.float32)


def expert_mix(rows, coef, gate_w, up_w, down_w):
    tokens, width = rows.shape
    experts, _, hidden = gate_w.shape
    flops = 6 * tokens * width * hidden * experts
    weight_bytes = 3 * experts * width * hidden * 2
    return pl.pallas_call(
        expert_kernel,
        grid=(experts,),
        out_shape=jax.ShapeDtypeStruct((tokens, width), jnp.float32),
        in_specs=[
            pl.BlockSpec((tokens, width), lambda e: (0, 0)),
            pl.BlockSpec((1, tokens, 1), lambda e: (e, 0, 0)),
            pl.BlockSpec((1, width, hidden), lambda e: (e, 0, 0)),
            pl.BlockSpec((1, width, hidden), lambda e: (e, 0, 0)),
            pl.BlockSpec((1, hidden, width), lambda e: (e, 0, 0)),
        ],
        out_specs=pl.BlockSpec((tokens, width), lambda e: (0, 0)),
        compiler_params=pltpu.CompilerParams(dimension_semantics=("arbitrary",)),
        cost_estimate=pl.CostEstimate(
            flops=flops,
            transcendentals=tokens * hidden * experts,
            bytes_accessed=weight_bytes + tokens * width * 6,
        ),
    )(rows, coef, gate_w, up_w, down_w)


def on_device(inputs, gain, w_gate, w_up, w_down, routes, shares):
    sections = lax.axis_size("section")
    shards = lax.axis_size("fsdp")
    chips = shards // 2
    section_index = lax.axis_index("section")
    core = lax.axis_index("fsdp") % 2
    micro, local, width = inputs.shape
    gain_row = gain[0]
    gate_w, up_w, down_w = w_gate[0], w_up[0], w_down[0]
    experts = gate_w.shape[0]
    coef = combine_weights(routes[0], shares[0], experts, shards)
    coef = coef.reshape(micro, experts, chips, 2, local)
    coef = jnp.concatenate(
        [
            lax.dynamic_index_in_dim(coef, core, 3, keepdims=False),
            lax.dynamic_index_in_dim(coef, 1 - core, 3, keepdims=False),
        ],
        axis=2,
    )
    coef = coef.reshape(micro, experts, shards * local, 1)
    output = jnp.zeros_like(inputs)
    carried = None
    for tick in range(micro + sections - 1):
        position = tick - section_index
        valid = jnp.logical_and(position >= 0, position < micro)
        clipped = jnp.clip(position, 0, micro - 1)
        entry = lax.dynamic_index_in_dim(inputs, clipped, 0, keepdims=False)
        coef_now = lax.dynamic_index_in_dim(coef, clipped, 0, keepdims=False)
        current = entry if carried is None else jnp.where(section_index == 0, entry, carried)
        normed = rms_norm(current, gain_row)
        lanes = local * width // 128
        near = exchange(normed.reshape(lanes, 128), chips, True, 0)
        rows = jnp.concatenate([near, sibling(near, "fsdp")], axis=0).reshape(shards * local, width)
        partial_value = expert_mix(rows, coef_now, gate_w, up_w, down_w).reshape(shards, local, width)
        chip_sum = partial_value[:chips] + sibling(partial_value[chips:], "fsdp")
        sent = chip_sum.astype(jnp.bfloat16).reshape(chips, lanes, 128)
        pieces = exchange(sent, chips, False, 1)
        mixed = jnp.sum(pieces.astype(jnp.float32), axis=0).reshape(local, width)
        result = (current.astype(jnp.float32) + mixed).astype(jnp.bfloat16)
        if tick + 1 < micro + sections - 1:
            carried = passed_along(result, "section", 1)
        updated = lax.dynamic_update_index_in_dim(output, result, clipped, 0)
        output = jnp.where(valid, updated, output)
    return output[None]


def solution(mesh):
    placed = (
        P(None, "fsdp", None),
        P("section", None),
        P("section", None, None, "fsdp"),
        P("section", None, None, "fsdp"),
        P("section", None, "fsdp", None),
        P("section", None, None, None),
        P("section", None, None, None),
    )
    return jax.shard_map(
        on_device,
        mesh=mesh,
        in_specs=placed,
        out_specs=P("section", None, "fsdp", None),
        check_vma=False,
    )
```

```python
import jax
import jax.numpy as jnp
from jax import lax
from jax.sharding import PartitionSpec as P
from jax.experimental import pallas as pl
from jax.experimental.pallas import tpu as pltpu

MESH = pl.DeviceIdType.MESH


def exchange(src, chips, same, collective_id):
    rows, width = src.shape[-2:]

    def kernel(src_ref, out_ref, send_sem, recv_sem, local_sem):
        me = lax.axis_index("fsdp")
        section = lax.axis_index("section")
        chip, core = me // 2, me % 2
        barrier = pltpu.get_barrier_semaphore()
        for j in range(1, chips):
            peer = lax.rem(chip + j, chips)
            pl.semaphore_signal(barrier, 1, device_id=(section, peer * 2 + core), device_id_type=MESH)
        pl.semaphore_wait(barrier, chips - 1)
        local = pltpu.make_async_copy(src_ref if same else src_ref.at[chip], out_ref.at[chip], local_sem)
        local.start()
        copies = []
        for j in range(1, chips):
            peer = lax.rem(chip + j, chips)
            copy = pltpu.make_async_remote_copy(
                src_ref=src_ref if same else src_ref.at[peer],
                dst_ref=out_ref.at[chip],
                send_sem=send_sem.at[j],
                recv_sem=recv_sem.at[j],
                device_id=(section, peer * 2 + core),
                device_id_type=MESH,
            )
            copy.start()
            copies.append(copy)
        local.wait()
        for copy in copies:
            copy.wait()

    return pl.pallas_call(
        kernel,
        out_shape=jax.ShapeDtypeStruct((chips, rows, width), src.dtype),
        in_specs=[pl.BlockSpec(memory_space=pl.ANY)],
        out_specs=pl.BlockSpec(memory_space=pl.ANY),
        scratch_shapes=[
            pltpu.SemaphoreType.DMA((chips,)),
            pltpu.SemaphoreType.DMA((chips,)),
            pltpu.SemaphoreType.DMA(()),
        ],
        compiler_params=pltpu.CompilerParams(collective_id=collective_id, has_side_effects=True),
    )(src)


def reduce_relay(sent, current, chips, sections, collective_id):
    _, rows, width = sent.shape

    def kernel(sent_ref, current_ref, result_ref, carried_ref, pieces, send_sem, recv_sem,
               local_sem, relay_send, relay_recv):
        me = lax.axis_index("fsdp")
        section = lax.axis_index("section")
        chip, core = me // 2, me % 2
        barrier = pltpu.get_barrier_semaphore()
        for j in range(1, chips):
            peer = lax.rem(chip + j, chips)
            pl.semaphore_signal(barrier, 1, device_id=(section, peer * 2 + core), device_id_type=MESH)

        @pl.when(section > 0)
        def _():
            pl.semaphore_signal(barrier, 1, device_id=(section - 1, me), device_id_type=MESH)

        has_next = (sections - 1 - section + sections - 2) // (sections - 1)
        pl.semaphore_wait(barrier, chips - 1 + has_next)

        local = pltpu.make_async_copy(sent_ref.at[chip], pieces.at[chip], local_sem)
        local.start()
        copies = []
        for j in range(1, chips):
            peer = lax.rem(chip + j, chips)
            copy = pltpu.make_async_remote_copy(
                src_ref=sent_ref.at[peer],
                dst_ref=pieces.at[chip],
                send_sem=send_sem.at[j],
                recv_sem=recv_sem.at[j],
                device_id=(section, peer * 2 + core),
                device_id_type=MESH,
            )
            copy.start()
            copies.append(copy)
        local.wait()
        for copy in copies:
            copy.wait()
        mixed = pieces[0].astype(jnp.float32)
        for k in range(1, chips):
            mixed = mixed + pieces[k].astype(jnp.float32)
        result_ref[...] = (current_ref[...].astype(jnp.float32) + mixed).astype(result_ref.dtype)
        relay = pltpu.make_async_remote_copy(
            src_ref=result_ref,
            dst_ref=carried_ref,
            send_sem=relay_send,
            recv_sem=relay_recv,
            device_id=(section + 1, me),
            device_id_type=MESH,
        )

        @pl.when(section < sections - 1)
        def _():
            relay.start()
            relay.wait_send()

        @pl.when(section > 0)
        def _():
            relay.wait_recv()

    vmem = pl.BlockSpec(memory_space=pltpu.VMEM)
    return pl.pallas_call(
        kernel,
        out_shape=(
            jax.ShapeDtypeStruct((rows, width), current.dtype),
            jax.ShapeDtypeStruct((rows, width), current.dtype),
        ),
        in_specs=[pl.BlockSpec(memory_space=pl.ANY), vmem],
        out_specs=(vmem, vmem),
        scratch_shapes=[
            pltpu.VMEM((chips, rows, width), sent.dtype),
            pltpu.SemaphoreType.DMA((chips,)),
            pltpu.SemaphoreType.DMA((chips,)),
            pltpu.SemaphoreType.DMA(()),
            pltpu.SemaphoreType.DMA(()),
            pltpu.SemaphoreType.DMA(()),
        ],
        compiler_params=pltpu.CompilerParams(collective_id=collective_id, has_side_effects=True),
    )(sent, current)


def passed_along(array, axis, by):
    devices = lax.axis_size(axis)
    pairs = [(i, i + by) for i in range(devices) if 0 <= i + by < devices]
    return lax.ppermute(array, axis, pairs)


def sibling(array, axis):
    devices = lax.axis_size(axis)
    return lax.ppermute(array, axis, [(i, i ^ 1) for i in range(devices)])


def rms_norm(rows, gain_row):
    values = rows.astype(jnp.float32)
    scale = lax.rsqrt(jnp.mean(values * values, axis=-1, keepdims=True) + 1e-05)
    return (values * scale * gain_row[None, :]).astype(jnp.bfloat16)


def combine_weights(route_layer, share_layer, experts, shards):
    micro, tokens, top = route_layer.shape
    per = tokens // shards
    onehot = (route_layer[..., None] == jnp.arange(experts, dtype=route_layer.dtype)).astype(jnp.float32)
    coef = jnp.sum(onehot * share_layer[..., None], axis=2)
    return coef.reshape(micro, shards, per, experts).transpose(0, 3, 1, 2)


def expert_mix(rows, coef, gate_w, up_w, down_w):
    gate = jnp.einsum("fmd,edh->efmh", rows, gate_w, preferred_element_type=jnp.float32)
    upward = jnp.einsum("fmd,edh->efmh", rows, up_w, preferred_element_type=jnp.float32)
    gated = (jax.nn.silu(gate) * upward * coef[..., None]).astype(jnp.bfloat16)
    return jnp.einsum("efmh,ehd->fmd", gated, down_w, preferred_element_type=jnp.float32)


def on_device(inputs, gain, w_gate, w_up, w_down, routes, shares):
    sections = lax.axis_size("section")
    shards = lax.axis_size("fsdp")
    chips = shards // 2
    section_index = lax.axis_index("section")
    core = lax.axis_index("fsdp") % 2
    micro, local, width = inputs.shape
    gain_row = gain[0]
    gate_w, up_w, down_w = w_gate[0], w_up[0], w_down[0]
    experts = gate_w.shape[0]
    coef = combine_weights(routes[0], shares[0], experts, shards)
    coef = coef.reshape(micro, experts, chips, 2, local)
    coef = jnp.concatenate(
        [
            lax.dynamic_index_in_dim(coef, core, 3, keepdims=False),
            lax.dynamic_index_in_dim(coef, 1 - core, 3, keepdims=False),
        ],
        axis=2,
    )
    output = jnp.zeros_like(inputs)
    carried = None
    for tick in range(micro + sections - 1):
        position = tick - section_index
        valid = jnp.logical_and(position >= 0, position < micro)
        clipped = jnp.clip(position, 0, micro - 1)
        entry = lax.dynamic_index_in_dim(inputs, clipped, 0, keepdims=False)
        coef_now = lax.dynamic_index_in_dim(coef, clipped, 0, keepdims=False)
        current = entry if carried is None else jnp.where(section_index == 0, entry, carried)
        normed = rms_norm(current, gain_row)
        lanes = local * width // 128
        near = exchange(normed.reshape(lanes, 128), chips, True, 0)
        rows = jnp.concatenate([near, sibling(near, "fsdp")], axis=0).reshape(shards, local, width)
        partial_value = expert_mix(rows, coef_now, gate_w, up_w, down_w)
        chip_sum = partial_value[:chips] + sibling(partial_value[chips:], "fsdp")
        sent = chip_sum.astype(jnp.bfloat16).reshape(chips, lanes, 128)
        result, carried = reduce_relay(sent, current.reshape(lanes, 128), chips, sections, 1)
        result = result.reshape(local, width)
        carried = carried.reshape(local, width)
        updated = lax.dynamic_update_index_in_dim(output, result, clipped, 0)
        output = jnp.where(valid, updated, output)
    return output[None]


def solution(mesh):
    placed = (
        P(None, "fsdp", None),
        P("section", None),
        P("section", None, None, "fsdp"),
        P("section", None, None, "fsdp"),
        P("section", None, "fsdp", None),
        P("section", None, None, None),
        P("section", None, None, None),
    )
    return jax.shard_map(
        on_device,
        mesh=mesh,
        in_specs=placed,
        out_specs=P("section", None, "fsdp", None),
        check_vma=False,
    )
```

```python
import jax
import jax.numpy as jnp
from jax import lax
from jax.sharding import PartitionSpec as P
from jax.experimental import pallas as pl
from jax.experimental.pallas import tpu as pltpu

MESH = pl.DeviceIdType.MESH


def exchange(src, chips, same, collective_id):
    rows, width = src.shape[-2:]

    def kernel(src_ref, out_ref, send_sem, recv_sem, local_sem):
        me = lax.axis_index("fsdp")
        section = lax.axis_index("section")
        chip, core = me // 2, me % 2
        barrier = pltpu.get_barrier_semaphore()
        for j in range(1, chips):
            peer = lax.rem(chip + j, chips)
            pl.semaphore_signal(barrier, 1, device_id=(section, peer * 2 + core), device_id_type=MESH)
        pl.semaphore_wait(barrier, chips - 1)
        local = pltpu.make_async_copy(src_ref if same else src_ref.at[chip], out_ref.at[chip], local_sem)
        local.start()
        copies = []
        for j in range(1, chips):
            peer = lax.rem(chip + j, chips)
            copy = pltpu.make_async_remote_copy(
                src_ref=src_ref if same else src_ref.at[peer],
                dst_ref=out_ref.at[chip],
                send_sem=send_sem.at[j],
                recv_sem=recv_sem.at[j],
                device_id=(section, peer * 2 + core),
                device_id_type=MESH,
            )
            copy.start()
            copies.append(copy)
        local.wait()
        for copy in copies:
            copy.wait()

    return pl.pallas_call(
        kernel,
        out_shape=jax.ShapeDtypeStruct((chips, rows, width), src.dtype),
        in_specs=[pl.BlockSpec(memory_space=pl.ANY)],
        out_specs=pl.BlockSpec(memory_space=pl.ANY),
        scratch_shapes=[
            pltpu.SemaphoreType.DMA((chips,)),
            pltpu.SemaphoreType.DMA((chips,)),
            pltpu.SemaphoreType.DMA(()),
        ],
        compiler_params=pltpu.CompilerParams(collective_id=collective_id, has_side_effects=True),
    )(src)


def gather_rows(src, chips, collective_id):
    rows, width = src.shape

    def kernel(src_ref, out_ref, send_sem, recv_sem, pass_send, pass_recv, local_sem):
        me = lax.axis_index("fsdp")
        section = lax.axis_index("section")
        chip, core = me // 2, me % 2
        partner = chip * 2 + 1 - core
        barrier = pltpu.get_barrier_semaphore()
        for j in range(1, chips):
            peer = lax.rem(chip + j, chips)
            pl.semaphore_signal(barrier, 1, device_id=(section, peer * 2 + core), device_id_type=MESH)
        pl.semaphore_signal(barrier, 1, device_id=(section, partner), device_id_type=MESH)
        pl.semaphore_wait(barrier, chips)
        local = pltpu.make_async_copy(src_ref, out_ref.at[chip], local_sem)
        local.start()
        copies = []
        for j in range(1, chips):
            peer = lax.rem(chip + j, chips)
            copy = pltpu.make_async_remote_copy(
                src_ref=src_ref,
                dst_ref=out_ref.at[chip],
                send_sem=send_sem.at[j],
                recv_sem=recv_sem.at[j],
                device_id=(section, peer * 2 + core),
                device_id_type=MESH,
            )
            copy.start()
            copies.append(copy)
        passes = []
        own = pltpu.make_async_remote_copy(
            src_ref=src_ref,
            dst_ref=out_ref.at[chips + chip],
            send_sem=pass_send.at[0],
            recv_sem=pass_recv.at[0],
            device_id=(section, partner),
            device_id_type=MESH,
        )
        own.start()
        passes.append(own)
        for j in range(1, chips):
            source = lax.rem(chip - j + chips, chips)
            copies[j - 1].wait_recv()
            onward = pltpu.make_async_remote_copy(
                src_ref=out_ref.at[source],
                dst_ref=out_ref.at[chips + source],
                send_sem=pass_send.at[j],
                recv_sem=pass_recv.at[j],
                device_id=(section, partner),
                device_id_type=MESH,
            )
            onward.start()
            passes.append(onward)
        local.wait()
        for copy in copies:
            copy.wait_send()
        for onward in passes:
            onward.wait()

    return pl.pallas_call(
        kernel,
        out_shape=jax.ShapeDtypeStruct((2 * chips, rows, width), src.dtype),
        in_specs=[pl.BlockSpec(memory_space=pl.ANY)],
        out_specs=pl.BlockSpec(memory_space=pl.ANY),
        scratch_shapes=[
            pltpu.SemaphoreType.DMA((chips,)),
            pltpu.SemaphoreType.DMA((chips,)),
            pltpu.SemaphoreType.DMA((chips,)),
            pltpu.SemaphoreType.DMA((chips,)),
            pltpu.SemaphoreType.DMA(()),
        ],
        compiler_params=pltpu.CompilerParams(collective_id=collective_id, has_side_effects=True),
    )(src)


def reduce_relay(sent, current, chips, sections, collective_id):
    _, rows, width = sent.shape

    def kernel(sent_ref, current_ref, result_ref, carried_ref, pieces, send_sem, recv_sem,
               local_sem, relay_send, relay_recv):
        me = lax.axis_index("fsdp")
        section = lax.axis_index("section")
        chip, core = me // 2, me % 2
        barrier = pltpu.get_barrier_semaphore()
        for j in range(1, chips):
            peer = lax.rem(chip + j, chips)
            pl.semaphore_signal(barrier, 1, device_id=(section, peer * 2 + core), device_id_type=MESH)

        @pl.when(section > 0)
        def _():
            pl.semaphore_signal(barrier, 1, device_id=(section - 1, me), device_id_type=MESH)

        has_next = (sections - 1 - section + sections - 2) // (sections - 1)
        pl.semaphore_wait(barrier, chips - 1 + has_next)

        local = pltpu.make_async_copy(sent_ref.at[chip], pieces.at[chip], local_sem)
        local.start()
        copies = []
        for j in range(1, chips):
            peer = lax.rem(chip + j, chips)
            copy = pltpu.make_async_remote_copy(
                src_ref=sent_ref.at[peer],
                dst_ref=pieces.at[chip],
                send_sem=send_sem.at[j],
                recv_sem=recv_sem.at[j],
                device_id=(section, peer * 2 + core),
                device_id_type=MESH,
            )
            copy.start()
            copies.append(copy)
        local.wait()
        for copy in copies:
            copy.wait()
        mixed = pieces[0].astype(jnp.float32)
        for k in range(1, chips):
            mixed = mixed + pieces[k].astype(jnp.float32)
        result_ref[...] = (current_ref[...].astype(jnp.float32) + mixed).astype(result_ref.dtype)
        relay = pltpu.make_async_remote_copy(
            src_ref=result_ref,
            dst_ref=carried_ref,
            send_sem=relay_send,
            recv_sem=relay_recv,
            device_id=(section + 1, me),
            device_id_type=MESH,
        )

        @pl.when(section < sections - 1)
        def _():
            relay.start()
            relay.wait_send()

        @pl.when(section > 0)
        def _():
            relay.wait_recv()

    vmem = pl.BlockSpec(memory_space=pltpu.VMEM)
    return pl.pallas_call(
        kernel,
        out_shape=(
            jax.ShapeDtypeStruct((rows, width), current.dtype),
            jax.ShapeDtypeStruct((rows, width), current.dtype),
        ),
        in_specs=[pl.BlockSpec(memory_space=pl.ANY), vmem],
        out_specs=(vmem, vmem),
        scratch_shapes=[
            pltpu.VMEM((chips, rows, width), sent.dtype),
            pltpu.SemaphoreType.DMA((chips,)),
            pltpu.SemaphoreType.DMA((chips,)),
            pltpu.SemaphoreType.DMA(()),
            pltpu.SemaphoreType.DMA(()),
            pltpu.SemaphoreType.DMA(()),
        ],
        compiler_params=pltpu.CompilerParams(collective_id=collective_id, has_side_effects=True),
    )(sent, current)


def passed_along(array, axis, by):
    devices = lax.axis_size(axis)
    pairs = [(i, i + by) for i in range(devices) if 0 <= i + by < devices]
    return lax.ppermute(array, axis, pairs)


def sibling(array, axis):
    devices = lax.axis_size(axis)
    return lax.ppermute(array, axis, [(i, i ^ 1) for i in range(devices)])


def rms_norm(rows, gain_row):
    values = rows.astype(jnp.float32)
    scale = lax.rsqrt(jnp.mean(values * values, axis=-1, keepdims=True) + 1e-05)
    return (values * scale * gain_row[None, :]).astype(jnp.bfloat16)


def combine_weights(route_layer, share_layer, experts, shards):
    micro, tokens, top = route_layer.shape
    per = tokens // shards
    onehot = (route_layer[..., None] == jnp.arange(experts, dtype=route_layer.dtype)).astype(jnp.float32)
    coef = jnp.sum(onehot * share_layer[..., None], axis=2)
    return coef.reshape(micro, shards, per, experts).transpose(0, 3, 1, 2)


def expert_mix(rows, coef, gate_w, up_w, down_w):
    gate = jnp.einsum("fmd,edh->efmh", rows, gate_w, preferred_element_type=jnp.float32)
    upward = jnp.einsum("fmd,edh->efmh", rows, up_w, preferred_element_type=jnp.float32)
    gated = (jax.nn.silu(gate) * upward * coef[..., None]).astype(jnp.bfloat16)
    return jnp.einsum("efmh,ehd->fmd", gated, down_w, preferred_element_type=jnp.float32)


def on_device(inputs, gain, w_gate, w_up, w_down, routes, shares):
    sections = lax.axis_size("section")
    shards = lax.axis_size("fsdp")
    chips = shards // 2
    section_index = lax.axis_index("section")
    core = lax.axis_index("fsdp") % 2
    micro, local, width = inputs.shape
    gain_row = gain[0]
    gate_w, up_w, down_w = w_gate[0], w_up[0], w_down[0]
    experts = gate_w.shape[0]
    coef = combine_weights(routes[0], shares[0], experts, shards)
    coef = coef.reshape(micro, experts, chips, 2, local)
    coef = jnp.concatenate(
        [
            lax.dynamic_index_in_dim(coef, core, 3, keepdims=False),
            lax.dynamic_index_in_dim(coef, 1 - core, 3, keepdims=False),
        ],
        axis=2,
    )
    output = jnp.zeros_like(inputs)
    carried = None
    for tick in range(micro + sections - 1):
        position = tick - section_index
        valid = jnp.logical_and(position >= 0, position < micro)
        clipped = jnp.clip(position, 0, micro - 1)
        entry = lax.dynamic_index_in_dim(inputs, clipped, 0, keepdims=False)
        coef_now = lax.dynamic_index_in_dim(coef, clipped, 0, keepdims=False)
        current = entry if carried is None else jnp.where(section_index == 0, entry, carried)
        normed = rms_norm(current, gain_row)
        lanes = local * width // 128
        rows = gather_rows(normed.reshape(lanes, 128), chips, 0).reshape(shards, local, width)
        partial_value = expert_mix(rows, coef_now, gate_w, up_w, down_w)
        chip_sum = partial_value[:chips] + sibling(partial_value[chips:], "fsdp")
        sent = chip_sum.astype(jnp.bfloat16).reshape(chips, lanes, 128)
        result, carried = reduce_relay(sent, current.reshape(lanes, 128), chips, sections, 1)
        result = result.reshape(local, width)
        carried = carried.reshape(local, width)
        updated = lax.dynamic_update_index_in_dim(output, result, clipped, 0)
        output = jnp.where(valid, updated, output)
    return output[None]


def solution(mesh):
    placed = (
        P(None, "fsdp", None),
        P("section", None),
        P("section", None, None, "fsdp"),
        P("section", None, None, "fsdp"),
        P("section", None, "fsdp", None),
        P("section", None, None, None),
        P("section", None, None, None),
    )
    return jax.shard_map(
        on_device,
        mesh=mesh,
        in_specs=placed,
        out_specs=P("section", None, "fsdp", None),
        check_vma=False,
    )
```

```python
import jax
import jax.numpy as jnp
from jax import lax
from jax.sharding import PartitionSpec as P
from jax.experimental import pallas as pl
from jax.experimental.pallas import tpu as pltpu

MESH = pl.DeviceIdType.MESH


def exchange(src, chips, same, collective_id):
    rows, width = src.shape[-2:]

    def kernel(src_ref, out_ref, send_sem, recv_sem, local_sem):
        me = lax.axis_index("fsdp")
        section = lax.axis_index("section")
        chip, core = me // 2, me % 2
        barrier = pltpu.get_barrier_semaphore()
        for j in range(1, chips):
            peer = lax.rem(chip + j, chips)
            pl.semaphore_signal(barrier, 1, device_id=(section, peer * 2 + core), device_id_type=MESH)
        pl.semaphore_wait(barrier, chips - 1)
        local = pltpu.make_async_copy(src_ref if same else src_ref.at[chip], out_ref.at[chip], local_sem)
        local.start()
        copies = []
        for j in range(1, chips):
            peer = lax.rem(chip + j, chips)
            copy = pltpu.make_async_remote_copy(
                src_ref=src_ref if same else src_ref.at[peer],
                dst_ref=out_ref.at[chip],
                send_sem=send_sem.at[j],
                recv_sem=recv_sem.at[j],
                device_id=(section, peer * 2 + core),
                device_id_type=MESH,
            )
            copy.start()
            copies.append(copy)
        local.wait()
        for copy in copies:
            copy.wait()

    return pl.pallas_call(
        kernel,
        out_shape=jax.ShapeDtypeStruct((chips, rows, width), src.dtype),
        in_specs=[pl.BlockSpec(memory_space=pl.ANY)],
        out_specs=pl.BlockSpec(memory_space=pl.ANY),
        scratch_shapes=[
            pltpu.SemaphoreType.DMA((chips,)),
            pltpu.SemaphoreType.DMA((chips,)),
            pltpu.SemaphoreType.DMA(()),
        ],
        compiler_params=pltpu.CompilerParams(collective_id=collective_id, has_side_effects=True),
    )(src)


def reduce_relay(sent, current, chips, sections, collective_id):
    _, rows, width = sent.shape

    def kernel(sent_ref, current_ref, result_ref, carried_ref, pieces, send_sem, recv_sem,
               local_sem, relay_send, relay_recv):
        me = lax.axis_index("fsdp")
        section = lax.axis_index("section")
        chip, core = me // 2, me % 2
        barrier = pltpu.get_barrier_semaphore()
        for j in range(1, chips):
            peer = lax.rem(chip + j, chips)
            pl.semaphore_signal(barrier, 1, device_id=(section, peer * 2 + core), device_id_type=MESH)

        @pl.when(section > 0)
        def _():
            pl.semaphore_signal(barrier, 1, device_id=(section - 1, me), device_id_type=MESH)

        has_next = (sections - 1 - section + sections - 2) // (sections - 1)
        pl.semaphore_wait(barrier, chips - 1 + has_next)

        local = pltpu.make_async_copy(sent_ref.at[chip], pieces.at[chip], local_sem)
        local.start()
        copies = []
        for j in range(1, chips):
            peer = lax.rem(chip + j, chips)
            copy = pltpu.make_async_remote_copy(
                src_ref=sent_ref.at[peer],
                dst_ref=pieces.at[chip],
                send_sem=send_sem.at[j],
                recv_sem=recv_sem.at[j],
                device_id=(section, peer * 2 + core),
                device_id_type=MESH,
            )
            copy.start()
            copies.append(copy)
        local.wait()
        for copy in copies:
            copy.wait()
        mixed = pieces[0].astype(jnp.float32)
        for k in range(1, chips):
            mixed = mixed + pieces[k].astype(jnp.float32)
        result_ref[...] = (current_ref[...].astype(jnp.float32) + mixed).astype(result_ref.dtype)
        relay = pltpu.make_async_remote_copy(
            src_ref=result_ref,
            dst_ref=carried_ref,
            send_sem=relay_send,
            recv_sem=relay_recv,
            device_id=(section + 1, me),
            device_id_type=MESH,
        )

        @pl.when(section < sections - 1)
        def _():
            relay.start()
            relay.wait_send()

        @pl.when(section > 0)
        def _():
            relay.wait_recv()

    vmem = pl.BlockSpec(memory_space=pltpu.VMEM)
    return pl.pallas_call(
        kernel,
        out_shape=(
            jax.ShapeDtypeStruct((rows, width), current.dtype),
            jax.ShapeDtypeStruct((rows, width), current.dtype),
        ),
        in_specs=[pl.BlockSpec(memory_space=pl.ANY), vmem],
        out_specs=(vmem, vmem),
        scratch_shapes=[
            pltpu.VMEM((chips, rows, width), sent.dtype),
            pltpu.SemaphoreType.DMA((chips,)),
            pltpu.SemaphoreType.DMA((chips,)),
            pltpu.SemaphoreType.DMA(()),
            pltpu.SemaphoreType.DMA(()),
            pltpu.SemaphoreType.DMA(()),
        ],
        compiler_params=pltpu.CompilerParams(collective_id=collective_id, has_side_effects=True),
    )(sent, current)


def passed_along(array, axis, by):
    devices = lax.axis_size(axis)
    pairs = [(i, i + by) for i in range(devices) if 0 <= i + by < devices]
    return lax.ppermute(array, axis, pairs)


def sibling(array, axis):
    devices = lax.axis_size(axis)
    return lax.ppermute(array, axis, [(i, i ^ 1) for i in range(devices)])


def rms_norm(rows, gain_row):
    values = rows.astype(jnp.float32)
    scale = lax.rsqrt(jnp.mean(values * values, axis=-1, keepdims=True) + 1e-05)
    return (values * scale * gain_row[None, :]).astype(jnp.bfloat16)


def combine_weights(route_layer, share_layer, experts, shards):
    micro, tokens, top = route_layer.shape
    per = tokens // shards
    onehot = (route_layer[..., None] == jnp.arange(experts, dtype=route_layer.dtype)).astype(jnp.float32)
    coef = jnp.sum(onehot * share_layer[..., None], axis=2)
    return coef.reshape(micro, shards, per, experts).transpose(0, 3, 1, 2)


def expert_mix(rows, coef, gate_w, up_w, down_w):
    gate = jnp.einsum("fmd,edh->efmh", rows, gate_w, preferred_element_type=jnp.float32)
    upward = jnp.einsum("fmd,edh->efmh", rows, up_w, preferred_element_type=jnp.float32)
    gated = (jax.nn.silu(gate) * upward * coef[..., None]).astype(jnp.bfloat16)
    return jnp.einsum("efmh,ehd->fmd", gated, down_w, preferred_element_type=jnp.float32)


def on_device(inputs, gain, w_gate, w_up, w_down, routes, shares):
    sections = lax.axis_size("section")
    shards = lax.axis_size("fsdp")
    chips = shards // 2
    section_index = lax.axis_index("section")
    core = lax.axis_index("fsdp") % 2
    micro, local, width = inputs.shape
    gain_row = gain[0]
    gate_w, up_w, down_w = w_gate[0], w_up[0], w_down[0]
    experts = gate_w.shape[0]
    coef = combine_weights(routes[0], shares[0], experts, shards)
    coef = coef.reshape(micro, experts, chips, 2, local)
    coef = jnp.concatenate(
        [
            lax.dynamic_index_in_dim(coef, core, 3, keepdims=False),
            lax.dynamic_index_in_dim(coef, 1 - core, 3, keepdims=False),
        ],
        axis=2,
    )
    output = jnp.zeros_like(inputs)
    carried = None
    for tick in range(micro + sections - 1):
        position = tick - section_index
        valid = jnp.logical_and(position >= 0, position < micro)
        clipped = jnp.clip(position, 0, micro - 1)
        entry = lax.dynamic_index_in_dim(inputs, clipped, 0, keepdims=False)
        coef_now = lax.dynamic_index_in_dim(coef, clipped, 0, keepdims=False)
        current = entry if carried is None else jnp.where(section_index == 0, entry, carried)
        normed = rms_norm(current, gain_row)
        lanes = local * width // 128
        near = exchange(normed.reshape(lanes, 128), chips, True, 0)
        rows = jnp.concatenate([near, sibling(near, "fsdp")], axis=0).reshape(shards, local, width)
        partial_value = expert_mix(rows, coef_now, gate_w, up_w, down_w)
        far_sum = sibling(partial_value[chips:].astype(jnp.bfloat16), "fsdp")
        chip_sum = partial_value[:chips] + far_sum.astype(jnp.float32)
        sent = chip_sum.astype(jnp.bfloat16).reshape(chips, lanes, 128)
        result, carried = reduce_relay(sent, current.reshape(lanes, 128), chips, sections, 1)
        result = result.reshape(local, width)
        carried = carried.reshape(local, width)
        updated = lax.dynamic_update_index_in_dim(output, result, clipped, 0)
        output = jnp.where(valid, updated, output)
    return output[None]


def solution(mesh):
    placed = (
        P(None, "fsdp", None),
        P("section", None),
        P("section", None, None, "fsdp"),
        P("section", None, None, "fsdp"),
        P("section", None, "fsdp", None),
        P("section", None, None, None),
        P("section", None, None, None),
    )
    return jax.shard_map(
        on_device,
        mesh=mesh,
        in_specs=placed,
        out_specs=P("section", None, "fsdp", None),
        check_vma=False,
    )
```

```python
import jax
import jax.numpy as jnp
from jax import lax
from jax.sharding import PartitionSpec as P
from jax.experimental import pallas as pl
from jax.experimental.pallas import tpu as pltpu

MESH = pl.DeviceIdType.MESH


def exchange(src, chips, same, collective_id):
    rows, width = src.shape[-2:]

    def kernel(src_ref, out_ref, send_sem, recv_sem, local_sem):
        me = lax.axis_index("fsdp")
        section = lax.axis_index("section")
        chip, core = me // 2, me % 2
        barrier = pltpu.get_barrier_semaphore()
        for j in range(1, chips):
            peer = lax.rem(chip + j, chips)
            pl.semaphore_signal(barrier, 1, device_id=(section, peer * 2 + core), device_id_type=MESH)
        pl.semaphore_wait(barrier, chips - 1)
        local = pltpu.make_async_copy(src_ref if same else src_ref.at[chip], out_ref.at[chip], local_sem)
        local.start()
        copies = []
        for j in range(1, chips):
            peer = lax.rem(chip + j, chips)
            copy = pltpu.make_async_remote_copy(
                src_ref=src_ref if same else src_ref.at[peer],
                dst_ref=out_ref.at[chip],
                send_sem=send_sem.at[j],
                recv_sem=recv_sem.at[j],
                device_id=(section, peer * 2 + core),
                device_id_type=MESH,
            )
            copy.start()
            copies.append(copy)
        local.wait()
        for copy in copies:
            copy.wait()

    return pl.pallas_call(
        kernel,
        out_shape=jax.ShapeDtypeStruct((chips, rows, width), src.dtype),
        in_specs=[pl.BlockSpec(memory_space=pl.ANY)],
        out_specs=pl.BlockSpec(memory_space=pl.ANY),
        scratch_shapes=[
            pltpu.SemaphoreType.DMA((chips,)),
            pltpu.SemaphoreType.DMA((chips,)),
            pltpu.SemaphoreType.DMA(()),
        ],
        compiler_params=pltpu.CompilerParams(collective_id=collective_id, has_side_effects=True),
    )(src)


def reduce_relay(sent, current, chips, sections, collective_id):
    _, rows, width = sent.shape

    def kernel(sent_ref, current_ref, result_ref, carried_ref, pieces, send_sem, recv_sem,
               local_sem, relay_send, relay_recv):
        me = lax.axis_index("fsdp")
        section = lax.axis_index("section")
        chip, core = me // 2, me % 2
        barrier = pltpu.get_barrier_semaphore()
        for j in range(1, chips):
            peer = lax.rem(chip + j, chips)
            pl.semaphore_signal(barrier, 1, device_id=(section, peer * 2 + core), device_id_type=MESH)

        @pl.when(section > 0)
        def _():
            pl.semaphore_signal(barrier, 1, device_id=(section - 1, me), device_id_type=MESH)

        has_next = (sections - 1 - section + sections - 2) // (sections - 1)
        pl.semaphore_wait(barrier, chips - 1 + has_next)

        local = pltpu.make_async_copy(sent_ref.at[chip], pieces.at[chip], local_sem)
        local.start()
        copies = []
        for j in range(1, chips):
            peer = lax.rem(chip + j, chips)
            copy = pltpu.make_async_remote_copy(
                src_ref=sent_ref.at[peer],
                dst_ref=pieces.at[chip],
                send_sem=send_sem.at[j],
                recv_sem=recv_sem.at[j],
                device_id=(section, peer * 2 + core),
                device_id_type=MESH,
            )
            copy.start()
            copies.append(copy)
        local.wait()
        for copy in copies:
            copy.wait()
        mixed = pieces[0].astype(jnp.float32)
        for k in range(1, chips):
            mixed = mixed + pieces[k].astype(jnp.float32)
        result_ref[...] = (current_ref[...].astype(jnp.float32) + mixed).astype(result_ref.dtype)
        relay = pltpu.make_async_remote_copy(
            src_ref=result_ref,
            dst_ref=carried_ref,
            send_sem=relay_send,
            recv_sem=relay_recv,
            device_id=(section + 1, me),
            device_id_type=MESH,
        )

        @pl.when(section < sections - 1)
        def _():
            relay.start()
            relay.wait_send()

        @pl.when(section > 0)
        def _():
            relay.wait_recv()

    vmem = pl.BlockSpec(memory_space=pltpu.VMEM)
    return pl.pallas_call(
        kernel,
        out_shape=(
            jax.ShapeDtypeStruct((rows, width), current.dtype),
            jax.ShapeDtypeStruct((rows, width), current.dtype),
        ),
        in_specs=[pl.BlockSpec(memory_space=pl.ANY), vmem],
        out_specs=(vmem, vmem),
        scratch_shapes=[
            pltpu.VMEM((chips, rows, width), sent.dtype),
            pltpu.SemaphoreType.DMA((chips,)),
            pltpu.SemaphoreType.DMA((chips,)),
            pltpu.SemaphoreType.DMA(()),
            pltpu.SemaphoreType.DMA(()),
            pltpu.SemaphoreType.DMA(()),
        ],
        compiler_params=pltpu.CompilerParams(collective_id=collective_id, has_side_effects=True),
    )(sent, current)


def passed_along(array, axis, by):
    devices = lax.axis_size(axis)
    pairs = [(i, i + by) for i in range(devices) if 0 <= i + by < devices]
    return lax.ppermute(array, axis, pairs)


def sibling(array, axis):
    devices = lax.axis_size(axis)
    return lax.ppermute(array, axis, [(i, i ^ 1) for i in range(devices)])


def rms_norm(rows, gain_row):
    values = rows.astype(jnp.float32)
    scale = lax.rsqrt(jnp.mean(values * values, axis=-1, keepdims=True) + 1e-05)
    return (values * scale * gain_row[None, :]).astype(jnp.bfloat16)


def combine_weights(route_layer, share_layer, experts, shards):
    micro, tokens, top = route_layer.shape
    per = tokens // shards
    onehot = (route_layer[..., None] == jnp.arange(experts, dtype=route_layer.dtype)).astype(jnp.float32)
    coef = jnp.sum(onehot * share_layer[..., None], axis=2)
    return coef.reshape(micro, shards, per, experts).transpose(0, 3, 1, 2)


def expert_mix(rows, coef, gate_w, up_w, down_w):
    gate = jnp.einsum("fmd,edh->fmeh", rows, gate_w, preferred_element_type=jnp.float32)
    upward = jnp.einsum("fmd,edh->fmeh", rows, up_w, preferred_element_type=jnp.float32)
    share = jnp.transpose(coef, (1, 2, 0))[..., None]
    gated = (jax.nn.silu(gate) * upward * share).astype(jnp.bfloat16)
    shards, local, experts, hidden = gated.shape
    gated = gated.reshape(shards, local, experts * hidden)
    down = down_w.reshape(experts * hidden, down_w.shape[2])
    return jnp.einsum("fmk,kd->fmd", gated, down, preferred_element_type=jnp.float32)


def on_device(inputs, gain, w_gate, w_up, w_down, routes, shares):
    sections = lax.axis_size("section")
    shards = lax.axis_size("fsdp")
    chips = shards // 2
    section_index = lax.axis_index("section")
    core = lax.axis_index("fsdp") % 2
    micro, local, width = inputs.shape
    gain_row = gain[0]
    gate_w, up_w, down_w = w_gate[0], w_up[0], w_down[0]
    experts = gate_w.shape[0]
    coef = combine_weights(routes[0], shares[0], experts, shards)
    coef = coef.reshape(micro, experts, chips, 2, local)
    coef = jnp.concatenate(
        [
            lax.dynamic_index_in_dim(coef, core, 3, keepdims=False),
            lax.dynamic_index_in_dim(coef, 1 - core, 3, keepdims=False),
        ],
        axis=2,
    )
    output = jnp.zeros_like(inputs)
    carried = None
    for tick in range(micro + sections - 1):
        position = tick - section_index
        valid = jnp.logical_and(position >= 0, position < micro)
        clipped = jnp.clip(position, 0, micro - 1)
        entry = lax.dynamic_index_in_dim(inputs, clipped, 0, keepdims=False)
        coef_now = lax.dynamic_index_in_dim(coef, clipped, 0, keepdims=False)
        current = entry if carried is None else jnp.where(section_index == 0, entry, carried)
        normed = rms_norm(current, gain_row)
        lanes = local * width // 128
        near = exchange(normed.reshape(lanes, 128), chips, True, 0)
        rows = jnp.concatenate([near, sibling(near, "fsdp")], axis=0).reshape(shards, local, width)
        partial_value = expert_mix(rows, coef_now, gate_w, up_w, down_w)
        far_sum = sibling(partial_value[chips:].astype(jnp.bfloat16), "fsdp")
        chip_sum = partial_value[:chips] + far_sum.astype(jnp.float32)
        sent = chip_sum.astype(jnp.bfloat16).reshape(chips, lanes, 128)
        result, carried = reduce_relay(sent, current.reshape(lanes, 128), chips, sections, 1)
        result = result.reshape(local, width)
        carried = carried.reshape(local, width)
        updated = lax.dynamic_update_index_in_dim(output, result, clipped, 0)
        output = jnp.where(valid, updated, output)
    return output[None]


def solution(mesh):
    placed = (
        P(None, "fsdp", None),
        P("section", None),
        P("section", None, None, "fsdp"),
        P("section", None, None, "fsdp"),
        P("section", None, "fsdp", None),
        P("section", None, None, None),
        P("section", None, None, None),
    )
    return jax.shard_map(
        on_device,
        mesh=mesh,
        in_specs=placed,
        out_specs=P("section", None, "fsdp", None),
        check_vma=False,
    )
```

```python
import jax
import jax.numpy as jnp
from jax import lax
from jax.sharding import PartitionSpec as P
from jax.experimental import pallas as pl
from jax.experimental.pallas import tpu as pltpu

MESH = pl.DeviceIdType.MESH


def exchange(src, chips, same, collective_id):
    rows, width = src.shape[-2:]

    def kernel(src_ref, out_ref, send_sem, recv_sem, local_sem):
        me = lax.axis_index("fsdp")
        section = lax.axis_index("section")
        chip, core = me // 2, me % 2
        barrier = pltpu.get_barrier_semaphore()
        for j in range(1, chips):
            peer = lax.rem(chip + j, chips)
            pl.semaphore_signal(barrier, 1, device_id=(section, peer * 2 + core), device_id_type=MESH)
        pl.semaphore_wait(barrier, chips - 1)
        local = pltpu.make_async_copy(src_ref if same else src_ref.at[chip], out_ref.at[chip], local_sem)
        local.start()
        copies = []
        for j in range(1, chips):
            peer = lax.rem(chip + j, chips)
            copy = pltpu.make_async_remote_copy(
                src_ref=src_ref if same else src_ref.at[peer],
                dst_ref=out_ref.at[chip],
                send_sem=send_sem.at[j],
                recv_sem=recv_sem.at[j],
                device_id=(section, peer * 2 + core),
                device_id_type=MESH,
            )
            copy.start()
            copies.append(copy)
        local.wait()
        for copy in copies:
            copy.wait()

    return pl.pallas_call(
        kernel,
        out_shape=jax.ShapeDtypeStruct((chips, rows, width), src.dtype),
        in_specs=[pl.BlockSpec(memory_space=pl.ANY)],
        out_specs=pl.BlockSpec(memory_space=pl.ANY),
        scratch_shapes=[
            pltpu.SemaphoreType.DMA((chips,)),
            pltpu.SemaphoreType.DMA((chips,)),
            pltpu.SemaphoreType.DMA(()),
        ],
        compiler_params=pltpu.CompilerParams(collective_id=collective_id, has_side_effects=True),
    )(src)


def reduce_relay(sent, current, chips, sections, collective_id):
    _, rows, width = sent.shape

    def kernel(sent_ref, current_ref, result_ref, carried_ref, pieces, send_sem, recv_sem,
               local_sem, relay_send, relay_recv):
        me = lax.axis_index("fsdp")
        section = lax.axis_index("section")
        chip, core = me // 2, me % 2
        barrier = pltpu.get_barrier_semaphore()
        for j in range(1, chips):
            peer = lax.rem(chip + j, chips)
            pl.semaphore_signal(barrier, 1, device_id=(section, peer * 2 + core), device_id_type=MESH)

        @pl.when(section > 0)
        def _():
            pl.semaphore_signal(barrier, 1, device_id=(section - 1, me), device_id_type=MESH)

        has_next = (sections - 1 - section + sections - 2) // (sections - 1)
        pl.semaphore_wait(barrier, chips - 1 + has_next)

        local = pltpu.make_async_copy(sent_ref.at[chip], pieces.at[chip], local_sem)
        local.start()
        copies = []
        for j in range(1, chips):
            peer = lax.rem(chip + j, chips)
            copy = pltpu.make_async_remote_copy(
                src_ref=sent_ref.at[peer],
                dst_ref=pieces.at[chip],
                send_sem=send_sem.at[j],
                recv_sem=recv_sem.at[j],
                device_id=(section, peer * 2 + core),
                device_id_type=MESH,
            )
            copy.start()
            copies.append(copy)
        local.wait()
        for copy in copies:
            copy.wait()
        mixed = pieces[0].astype(jnp.float32)
        for k in range(1, chips):
            mixed = mixed + pieces[k].astype(jnp.float32)
        result_ref[...] = (current_ref[...].astype(jnp.float32) + mixed).astype(result_ref.dtype)
        relay = pltpu.make_async_remote_copy(
            src_ref=result_ref,
            dst_ref=carried_ref,
            send_sem=relay_send,
            recv_sem=relay_recv,
            device_id=(section + 1, me),
            device_id_type=MESH,
        )

        @pl.when(section < sections - 1)
        def _():
            relay.start()
            relay.wait_send()

        @pl.when(section > 0)
        def _():
            relay.wait_recv()

    vmem = pl.BlockSpec(memory_space=pltpu.VMEM)
    return pl.pallas_call(
        kernel,
        out_shape=(
            jax.ShapeDtypeStruct((rows, width), current.dtype),
            jax.ShapeDtypeStruct((rows, width), current.dtype),
        ),
        in_specs=[pl.BlockSpec(memory_space=pl.ANY), vmem],
        out_specs=(vmem, vmem),
        scratch_shapes=[
            pltpu.VMEM((chips, rows, width), sent.dtype),
            pltpu.SemaphoreType.DMA((chips,)),
            pltpu.SemaphoreType.DMA((chips,)),
            pltpu.SemaphoreType.DMA(()),
            pltpu.SemaphoreType.DMA(()),
            pltpu.SemaphoreType.DMA(()),
        ],
        compiler_params=pltpu.CompilerParams(collective_id=collective_id, has_side_effects=True),
    )(sent, current)


def passed_along(array, axis, by):
    devices = lax.axis_size(axis)
    pairs = [(i, i + by) for i in range(devices) if 0 <= i + by < devices]
    return lax.ppermute(array, axis, pairs)


def sibling(array, axis):
    devices = lax.axis_size(axis)
    return lax.ppermute(array, axis, [(i, i ^ 1) for i in range(devices)])


def rms_norm(rows, gain_row):
    values = rows.astype(jnp.float32)
    scale = lax.rsqrt(jnp.mean(values * values, axis=-1, keepdims=True) + 1e-05)
    return (values * scale * gain_row[None, :]).astype(jnp.bfloat16)


def combine_weights(route_layer, share_layer, experts, shards):
    micro, tokens, top = route_layer.shape
    per = tokens // shards
    onehot = (route_layer[..., None] == jnp.arange(experts, dtype=route_layer.dtype)).astype(jnp.float32)
    coef = jnp.sum(onehot * share_layer[..., None], axis=2)
    return coef.reshape(micro, shards, per, experts).transpose(0, 3, 1, 2)


def expert_mix(rows, coef, gate_w, up_w, down_w):
    gate = jnp.einsum("fmd,edh->fmeh", rows, gate_w, preferred_element_type=jnp.float32)
    upward = jnp.einsum("fmd,edh->fmeh", rows, up_w, preferred_element_type=jnp.float32)
    share = jnp.transpose(coef, (1, 2, 0))[..., None]
    gated = (jax.nn.silu(gate) * upward * share).astype(jnp.bfloat16)
    shards, local, experts, hidden = gated.shape
    gated = gated.reshape(shards, local, experts * hidden)
    down = down_w.reshape(experts * hidden, down_w.shape[2])
    return jnp.einsum("fmk,kd->fmd", gated, down, preferred_element_type=jnp.float32)


def on_device(inputs, gain, w_gate, w_up, w_down, routes, shares):
    sections = lax.axis_size("section")
    shards = lax.axis_size("fsdp")
    chips = shards // 2
    section_index = lax.axis_index("section")
    core = lax.axis_index("fsdp") % 2
    micro, local, width = inputs.shape
    gain_row = gain[0]
    gate_w, up_w, down_w = w_gate[0], w_up[0], w_down[0]
    experts = gate_w.shape[0]
    coef = combine_weights(routes[0], shares[0], experts, shards)
    coef = coef.reshape(micro, experts, chips, 2, local)
    coef = jnp.concatenate(
        [
            lax.dynamic_index_in_dim(coef, core, 3, keepdims=False),
            lax.dynamic_index_in_dim(coef, 1 - core, 3, keepdims=False),
        ],
        axis=2,
    )
    lanes = local * width // 128
    flat_inputs = inputs.reshape(micro, lanes, 128)
    output = jnp.zeros_like(flat_inputs)
    carried = None
    for tick in range(micro + sections - 1):
        position = tick - section_index
        valid = jnp.logical_and(position >= 0, position < micro)
        clipped = jnp.clip(position, 0, micro - 1)
        entry = lax.dynamic_index_in_dim(flat_inputs, clipped, 0, keepdims=False)
        coef_now = lax.dynamic_index_in_dim(coef, clipped, 0, keepdims=False)
        current = entry if carried is None else jnp.where(section_index == 0, entry, carried)
        normed = rms_norm(current.reshape(local, width), gain_row)
        near = exchange(normed.reshape(lanes, 128), chips, True, 0)
        rows = jnp.concatenate([near, sibling(near, "fsdp")], axis=0).reshape(shards, local, width)
        partial_value = expert_mix(rows, coef_now, gate_w, up_w, down_w)
        far_sum = sibling(partial_value[chips:].astype(jnp.bfloat16), "fsdp")
        chip_sum = partial_value[:chips] + far_sum.astype(jnp.float32)
        sent = chip_sum.astype(jnp.bfloat16).reshape(chips, lanes, 128)
        result, carried = reduce_relay(sent, current, chips, sections, 1)
        updated = lax.dynamic_update_index_in_dim(output, result, clipped, 0)
        output = jnp.where(valid, updated, output)
    return output.reshape(1, micro, local, width)


def solution(mesh):
    placed = (
        P(None, "fsdp", None),
        P("section", None),
        P("section", None, None, "fsdp"),
        P("section", None, None, "fsdp"),
        P("section", None, "fsdp", None),
        P("section", None, None, None),
        P("section", None, None, None),
    )
    return jax.shard_map(
        on_device,
        mesh=mesh,
        in_specs=placed,
        out_specs=P("section", None, "fsdp", None),
        check_vma=False,
    )
```

```python
import jax
import jax.numpy as jnp
from jax import lax
from jax.sharding import PartitionSpec as P
from jax.experimental import pallas as pl
from jax.experimental.pallas import tpu as pltpu

MESH = pl.DeviceIdType.MESH


def exchange(src, chips, same, collective_id):
    rows, width = src.shape[-2:]

    def kernel(src_ref, out_ref, send_sem, recv_sem, local_sem):
        me = lax.axis_index("fsdp")
        section = lax.axis_index("section")
        chip, core = me // 2, me % 2
        barrier = pltpu.get_barrier_semaphore()
        for j in range(1, chips):
            peer = lax.rem(chip + j, chips)
            pl.semaphore_signal(barrier, 1, device_id=(section, peer * 2 + core), device_id_type=MESH)
        pl.semaphore_wait(barrier, chips - 1)
        local = pltpu.make_async_copy(src_ref if same else src_ref.at[chip], out_ref.at[chip], local_sem)
        local.start()
        copies = []
        for j in range(1, chips):
            peer = lax.rem(chip + j, chips)
            copy = pltpu.make_async_remote_copy(
                src_ref=src_ref if same else src_ref.at[peer],
                dst_ref=out_ref.at[chip],
                send_sem=send_sem.at[j],
                recv_sem=recv_sem.at[j],
                device_id=(section, peer * 2 + core),
                device_id_type=MESH,
            )
            copy.start()
            copies.append(copy)
        local.wait()
        for copy in copies:
            copy.wait()

    return pl.pallas_call(
        kernel,
        out_shape=jax.ShapeDtypeStruct((chips, rows, width), src.dtype),
        in_specs=[pl.BlockSpec(memory_space=pl.ANY)],
        out_specs=pl.BlockSpec(memory_space=pl.ANY),
        scratch_shapes=[
            pltpu.SemaphoreType.DMA((chips,)),
            pltpu.SemaphoreType.DMA((chips,)),
            pltpu.SemaphoreType.DMA(()),
        ],
        compiler_params=pltpu.CompilerParams(collective_id=collective_id, has_side_effects=True),
    )(src)


def reduce_relay(sent, current, chips, sections, collective_id):
    _, rows, width = sent.shape

    def kernel(sent_ref, current_ref, result_ref, carried_ref, pieces, send_sem, recv_sem,
               local_sem, relay_send, relay_recv):
        me = lax.axis_index("fsdp")
        section = lax.axis_index("section")
        chip, core = me // 2, me % 2
        barrier = pltpu.get_barrier_semaphore()
        for j in range(1, chips):
            peer = lax.rem(chip + j, chips)
            pl.semaphore_signal(barrier, 1, device_id=(section, peer * 2 + core), device_id_type=MESH)

        @pl.when(section > 0)
        def _():
            pl.semaphore_signal(barrier, 1, device_id=(section - 1, me), device_id_type=MESH)

        has_next = (sections - 1 - section + sections - 2) // (sections - 1)
        pl.semaphore_wait(barrier, chips - 1 + has_next)

        local = pltpu.make_async_copy(sent_ref.at[chip], pieces.at[chip], local_sem)
        local.start()
        copies = []
        for j in range(1, chips):
            peer = lax.rem(chip + j, chips)
            copy = pltpu.make_async_remote_copy(
                src_ref=sent_ref.at[peer],
                dst_ref=pieces.at[chip],
                send_sem=send_sem.at[j],
                recv_sem=recv_sem.at[j],
                device_id=(section, peer * 2 + core),
                device_id_type=MESH,
            )
            copy.start()
            copies.append(copy)
        local.wait()
        for copy in copies:
            copy.wait()
        mixed = pieces[0].astype(jnp.float32)
        for k in range(1, chips):
            mixed = mixed + pieces[k].astype(jnp.float32)
        result_ref[...] = (current_ref[...].astype(jnp.float32) + mixed).astype(result_ref.dtype)
        relay = pltpu.make_async_remote_copy(
            src_ref=result_ref,
            dst_ref=carried_ref,
            send_sem=relay_send,
            recv_sem=relay_recv,
            device_id=(section + 1, me),
            device_id_type=MESH,
        )

        @pl.when(section < sections - 1)
        def _():
            relay.start()
            relay.wait_send()

        @pl.when(section > 0)
        def _():
            relay.wait_recv()

    vmem = pl.BlockSpec(memory_space=pltpu.VMEM)
    return pl.pallas_call(
        kernel,
        out_shape=(
            jax.ShapeDtypeStruct((rows, width), current.dtype),
            jax.ShapeDtypeStruct((rows, width), current.dtype),
        ),
        in_specs=[pl.BlockSpec(memory_space=pl.ANY), vmem],
        out_specs=(vmem, vmem),
        scratch_shapes=[
            pltpu.VMEM((chips, rows, width), sent.dtype),
            pltpu.SemaphoreType.DMA((chips,)),
            pltpu.SemaphoreType.DMA((chips,)),
            pltpu.SemaphoreType.DMA(()),
            pltpu.SemaphoreType.DMA(()),
            pltpu.SemaphoreType.DMA(()),
        ],
        compiler_params=pltpu.CompilerParams(collective_id=collective_id, has_side_effects=True),
    )(sent, current)


def passed_along(array, axis, by):
    devices = lax.axis_size(axis)
    pairs = [(i, i + by) for i in range(devices) if 0 <= i + by < devices]
    return lax.ppermute(array, axis, pairs)


def sibling(array, axis):
    devices = lax.axis_size(axis)
    return lax.ppermute(array, axis, [(i, i ^ 1) for i in range(devices)])


def rms_norm(rows, gain_row):
    values = rows.astype(jnp.float32)
    scale = lax.rsqrt(jnp.mean(values * values, axis=-1, keepdims=True) + 1e-05)
    return (values * scale * gain_row[None, :]).astype(jnp.bfloat16)


def rms_norm_lanes(rows, gain_lanes, tokens):
    values = rows.astype(jnp.float32)
    per_row = jnp.sum(values * values, axis=1)
    per_token = jnp.sum(per_row.reshape(tokens, -1), axis=1)
    width = rows.size // tokens
    scale = lax.rsqrt(per_token / width + 1e-05)
    scale_rows = jnp.repeat(scale, rows.shape[0] // tokens)
    return (values * scale_rows[:, None] * gain_lanes).astype(jnp.bfloat16)


def combine_weights(route_layer, share_layer, experts, shards):
    micro, tokens, top = route_layer.shape
    per = tokens // shards
    onehot = (route_layer[..., None] == jnp.arange(experts, dtype=route_layer.dtype)).astype(jnp.float32)
    coef = jnp.sum(onehot * share_layer[..., None], axis=2)
    return coef.reshape(micro, shards, per, experts).transpose(0, 3, 1, 2)


def expert_mix(rows, coef, gate_w, up_w, down_w):
    gate = jnp.einsum("fmd,edh->fmeh", rows, gate_w, preferred_element_type=jnp.float32)
    upward = jnp.einsum("fmd,edh->fmeh", rows, up_w, preferred_element_type=jnp.float32)
    share = jnp.transpose(coef, (1, 2, 0))[..., None]
    gated = (jax.nn.silu(gate) * upward * share).astype(jnp.bfloat16)
    shards, local, experts, hidden = gated.shape
    gated = gated.reshape(shards, local, experts * hidden)
    down = down_w.reshape(experts * hidden, down_w.shape[2])
    return jnp.einsum("fmk,kd->fmd", gated, down, preferred_element_type=jnp.float32)


def on_device(inputs, gain, w_gate, w_up, w_down, routes, shares):
    sections = lax.axis_size("section")
    shards = lax.axis_size("fsdp")
    chips = shards // 2
    section_index = lax.axis_index("section")
    core = lax.axis_index("fsdp") % 2
    micro, local, width = inputs.shape
    gain_row = gain[0]
    gate_w, up_w, down_w = w_gate[0], w_up[0], w_down[0]
    experts = gate_w.shape[0]
    coef = combine_weights(routes[0], shares[0], experts, shards)
    coef = coef.reshape(micro, experts, chips, 2, local)
    coef = jnp.concatenate(
        [
            lax.dynamic_index_in_dim(coef, core, 3, keepdims=False),
            lax.dynamic_index_in_dim(coef, 1 - core, 3, keepdims=False),
        ],
        axis=2,
    )
    lanes = local * width // 128
    gain_lanes = jnp.tile(gain_row.reshape(lanes // local, 128), (local, 1))
    flat_inputs = inputs.reshape(micro, lanes, 128)
    output = jnp.zeros_like(flat_inputs)
    carried = None
    for tick in range(micro + sections - 1):
        position = tick - section_index
        valid = jnp.logical_and(position >= 0, position < micro)
        clipped = jnp.clip(position, 0, micro - 1)
        entry = lax.dynamic_index_in_dim(flat_inputs, clipped, 0, keepdims=False)
        coef_now = lax.dynamic_index_in_dim(coef, clipped, 0, keepdims=False)
        current = entry if carried is None else jnp.where(section_index == 0, entry, carried)
        normed = rms_norm_lanes(current, gain_lanes, local)
        near = exchange(normed, chips, True, 0)
        rows = jnp.concatenate([near, sibling(near, "fsdp")], axis=0).reshape(shards, local, width)
        partial_value = expert_mix(rows, coef_now, gate_w, up_w, down_w)
        far_sum = sibling(partial_value[chips:].astype(jnp.bfloat16), "fsdp")
        chip_sum = partial_value[:chips] + far_sum.astype(jnp.float32)
        sent = chip_sum.astype(jnp.bfloat16).reshape(chips, lanes, 128)
        result, carried = reduce_relay(sent, current, chips, sections, 1)
        updated = lax.dynamic_update_index_in_dim(output, result, clipped, 0)
        output = jnp.where(valid, updated, output)
    return output.reshape(1, micro, local, width)


def solution(mesh):
    placed = (
        P(None, "fsdp", None),
        P("section", None),
        P("section", None, None, "fsdp"),
        P("section", None, None, "fsdp"),
        P("section", None, "fsdp", None),
        P("section", None, None, None),
        P("section", None, None, None),
    )
    return jax.shard_map(
        on_device,
        mesh=mesh,
        in_specs=placed,
        out_specs=P("section", None, "fsdp", None),
        check_vma=False,
    )
```

```python
import jax
import jax.numpy as jnp
from jax import lax
from jax.sharding import PartitionSpec as P
from jax.experimental import pallas as pl
from jax.experimental.pallas import tpu as pltpu

MESH = pl.DeviceIdType.MESH


def exchange(src, chips, same, collective_id):
    rows, width = src.shape[-2:]

    def kernel(src_ref, out_ref, send_sem, recv_sem, local_sem):
        me = lax.axis_index("fsdp")
        section = lax.axis_index("section")
        chip, core = me // 2, me % 2
        barrier = pltpu.get_barrier_semaphore()
        for j in range(1, chips):
            peer = lax.rem(chip + j, chips)
            pl.semaphore_signal(barrier, 1, device_id=(section, peer * 2 + core), device_id_type=MESH)
        pl.semaphore_wait(barrier, chips - 1)
        local = pltpu.make_async_copy(src_ref if same else src_ref.at[chip], out_ref.at[chip], local_sem)
        local.start()
        copies = []
        for j in range(1, chips):
            peer = lax.rem(chip + j, chips)
            copy = pltpu.make_async_remote_copy(
                src_ref=src_ref if same else src_ref.at[peer],
                dst_ref=out_ref.at[chip],
                send_sem=send_sem.at[j],
                recv_sem=recv_sem.at[j],
                device_id=(section, peer * 2 + core),
                device_id_type=MESH,
            )
            copy.start()
            copies.append(copy)
        local.wait()
        for copy in copies:
            copy.wait()

    return pl.pallas_call(
        kernel,
        out_shape=jax.ShapeDtypeStruct((chips, rows, width), src.dtype),
        in_specs=[pl.BlockSpec(memory_space=pl.ANY)],
        out_specs=pl.BlockSpec(memory_space=pl.ANY),
        scratch_shapes=[
            pltpu.SemaphoreType.DMA((chips,)),
            pltpu.SemaphoreType.DMA((chips,)),
            pltpu.SemaphoreType.DMA(()),
        ],
        compiler_params=pltpu.CompilerParams(collective_id=collective_id, has_side_effects=True),
    )(src)


def reduce_relay(sent, current, chips, sections, collective_id):
    _, rows, width = sent.shape

    def kernel(sent_ref, current_ref, result_ref, carried_ref, pieces, send_sem, recv_sem,
               local_sem, relay_send, relay_recv):
        me = lax.axis_index("fsdp")
        section = lax.axis_index("section")
        chip, core = me // 2, me % 2
        barrier = pltpu.get_barrier_semaphore()
        for j in range(1, chips):
            peer = lax.rem(chip + j, chips)
            pl.semaphore_signal(barrier, 1, device_id=(section, peer * 2 + core), device_id_type=MESH)

        @pl.when(section > 0)
        def _():
            pl.semaphore_signal(barrier, 1, device_id=(section - 1, me), device_id_type=MESH)

        has_next = (sections - 1 - section + sections - 2) // (sections - 1)
        pl.semaphore_wait(barrier, chips - 1 + has_next)

        local = pltpu.make_async_copy(sent_ref.at[chip], pieces.at[chip], local_sem)
        local.start()
        copies = []
        for j in range(1, chips):
            peer = lax.rem(chip + j, chips)
            copy = pltpu.make_async_remote_copy(
                src_ref=sent_ref.at[peer],
                dst_ref=pieces.at[chip],
                send_sem=send_sem.at[j],
                recv_sem=recv_sem.at[j],
                device_id=(section, peer * 2 + core),
                device_id_type=MESH,
            )
            copy.start()
            copies.append(copy)
        local.wait()
        mixed = pieces[chip].astype(jnp.float32)
        for j, copy in enumerate(copies, start=1):
            copy.wait_recv()
            mixed = mixed + pieces[lax.rem(chip - j + chips, chips)].astype(jnp.float32)
        for copy in copies:
            copy.wait_send()
        result_ref[...] = (current_ref[...].astype(jnp.float32) + mixed).astype(result_ref.dtype)
        relay = pltpu.make_async_remote_copy(
            src_ref=result_ref,
            dst_ref=carried_ref,
            send_sem=relay_send,
            recv_sem=relay_recv,
            device_id=(section + 1, me),
            device_id_type=MESH,
        )

        @pl.when(section < sections - 1)
        def _():
            relay.start()
            relay.wait_send()

        @pl.when(section > 0)
        def _():
            relay.wait_recv()

    vmem = pl.BlockSpec(memory_space=pltpu.VMEM)
    return pl.pallas_call(
        kernel,
        out_shape=(
            jax.ShapeDtypeStruct((rows, width), current.dtype),
            jax.ShapeDtypeStruct((rows, width), current.dtype),
        ),
        in_specs=[pl.BlockSpec(memory_space=pl.ANY), vmem],
        out_specs=(vmem, vmem),
        scratch_shapes=[
            pltpu.VMEM((chips, rows, width), sent.dtype),
            pltpu.SemaphoreType.DMA((chips,)),
            pltpu.SemaphoreType.DMA((chips,)),
            pltpu.SemaphoreType.DMA(()),
            pltpu.SemaphoreType.DMA(()),
            pltpu.SemaphoreType.DMA(()),
        ],
        compiler_params=pltpu.CompilerParams(collective_id=collective_id, has_side_effects=True),
    )(sent, current)


def passed_along(array, axis, by):
    devices = lax.axis_size(axis)
    pairs = [(i, i + by) for i in range(devices) if 0 <= i + by < devices]
    return lax.ppermute(array, axis, pairs)


def sibling(array, axis):
    devices = lax.axis_size(axis)
    return lax.ppermute(array, axis, [(i, i ^ 1) for i in range(devices)])


def rms_norm(rows, gain_row):
    values = rows.astype(jnp.float32)
    scale = lax.rsqrt(jnp.mean(values * values, axis=-1, keepdims=True) + 1e-05)
    return (values * scale * gain_row[None, :]).astype(jnp.bfloat16)


def combine_weights(route_layer, share_layer, experts, shards):
    micro, tokens, top = route_layer.shape
    per = tokens // shards
    onehot = (route_layer[..., None] == jnp.arange(experts, dtype=route_layer.dtype)).astype(jnp.float32)
    coef = jnp.sum(onehot * share_layer[..., None], axis=2)
    return coef.reshape(micro, shards, per, experts).transpose(0, 3, 1, 2)


def expert_mix(rows, coef, gate_w, up_w, down_w):
    gate = jnp.einsum("fmd,edh->fmeh", rows, gate_w, preferred_element_type=jnp.float32)
    upward = jnp.einsum("fmd,edh->fmeh", rows, up_w, preferred_element_type=jnp.float32)
    share = jnp.transpose(coef, (1, 2, 0))[..., None]
    gated = (jax.nn.silu(gate) * upward * share).astype(jnp.bfloat16)
    shards, local, experts, hidden = gated.shape
    gated = gated.reshape(shards, local, experts * hidden)
    down = down_w.reshape(experts * hidden, down_w.shape[2])
    return jnp.einsum("fmk,kd->fmd", gated, down, preferred_element_type=jnp.float32)


def on_device(inputs, gain, w_gate, w_up, w_down, routes, shares):
    sections = lax.axis_size("section")
    shards = lax.axis_size("fsdp")
    chips = shards // 2
    section_index = lax.axis_index("section")
    core = lax.axis_index("fsdp") % 2
    micro, local, width = inputs.shape
    gain_row = gain[0]
    gate_w, up_w, down_w = w_gate[0], w_up[0], w_down[0]
    experts = gate_w.shape[0]
    coef = combine_weights(routes[0], shares[0], experts, shards)
    coef = coef.reshape(micro, experts, chips, 2, local)
    coef = jnp.concatenate(
        [
            lax.dynamic_index_in_dim(coef, core, 3, keepdims=False),
            lax.dynamic_index_in_dim(coef, 1 - core, 3, keepdims=False),
        ],
        axis=2,
    )
    lanes = local * width // 128
    flat_inputs = inputs.reshape(micro, lanes, 128)
    output = jnp.zeros_like(flat_inputs)
    carried = None
    for tick in range(micro + sections - 1):
        position = tick - section_index
        valid = jnp.logical_and(position >= 0, position < micro)
        clipped = jnp.clip(position, 0, micro - 1)
        entry = lax.dynamic_index_in_dim(flat_inputs, clipped, 0, keepdims=False)
        coef_now = lax.dynamic_index_in_dim(coef, clipped, 0, keepdims=False)
        current = entry if carried is None else jnp.where(section_index == 0, entry, carried)
        normed = rms_norm(current.reshape(local, width), gain_row)
        near = exchange(normed.reshape(lanes, 128), chips, True, 0)
        rows = jnp.concatenate([near, sibling(near, "fsdp")], axis=0).reshape(shards, local, width)
        partial_value = expert_mix(rows, coef_now, gate_w, up_w, down_w)
        far_sum = sibling(partial_value[chips:].astype(jnp.bfloat16), "fsdp")
        chip_sum = partial_value[:chips] + far_sum.astype(jnp.float32)
        sent = chip_sum.astype(jnp.bfloat16).reshape(chips, lanes, 128)
        result, carried = reduce_relay(sent, current, chips, sections, 1)
        updated = lax.dynamic_update_index_in_dim(output, result, clipped, 0)
        output = jnp.where(valid, updated, output)
    return output.reshape(1, micro, local, width)


def solution(mesh):
    placed = (
        P(None, "fsdp", None),
        P("section", None),
        P("section", None, None, "fsdp"),
        P("section", None, None, "fsdp"),
        P("section", None, "fsdp", None),
        P("section", None, None, None),
        P("section", None, None, None),
    )
    return jax.shard_map(
        on_device,
        mesh=mesh,
        in_specs=placed,
        out_specs=P("section", None, "fsdp", None),
        check_vma=False,
    )
```

```python
import jax
import jax.numpy as jnp
from jax import lax
from jax.sharding import PartitionSpec as P
from jax.experimental import pallas as pl
from jax.experimental.pallas import tpu as pltpu

MESH = pl.DeviceIdType.MESH


def exchange(src, chips, same, collective_id):
    rows, width = src.shape[-2:]

    def kernel(src_ref, out_ref, send_sem, recv_sem, local_sem):
        me = lax.axis_index("fsdp")
        section = lax.axis_index("section")
        chip, core = me // 2, me % 2
        barrier = pltpu.get_barrier_semaphore()
        for j in range(1, chips):
            peer = lax.rem(chip + j, chips)
            pl.semaphore_signal(barrier, 1, device_id=(section, peer * 2 + core), device_id_type=MESH)
        pl.semaphore_wait(barrier, chips - 1)
        local = pltpu.make_async_copy(src_ref if same else src_ref.at[chip], out_ref.at[chip], local_sem)
        local.start()
        copies = []
        for j in range(1, chips):
            peer = lax.rem(chip + j, chips)
            copy = pltpu.make_async_remote_copy(
                src_ref=src_ref if same else src_ref.at[peer],
                dst_ref=out_ref.at[chip],
                send_sem=send_sem.at[j],
                recv_sem=recv_sem.at[j],
                device_id=(section, peer * 2 + core),
                device_id_type=MESH,
            )
            copy.start()
            copies.append(copy)
        local.wait()
        for copy in copies:
            copy.wait()

    return pl.pallas_call(
        kernel,
        out_shape=jax.ShapeDtypeStruct((chips, rows, width), src.dtype),
        in_specs=[pl.BlockSpec(memory_space=pl.ANY)],
        out_specs=pl.BlockSpec(memory_space=pl.ANY),
        scratch_shapes=[
            pltpu.SemaphoreType.DMA((chips,)),
            pltpu.SemaphoreType.DMA((chips,)),
            pltpu.SemaphoreType.DMA(()),
        ],
        compiler_params=pltpu.CompilerParams(collective_id=collective_id, has_side_effects=True),
    )(src)


def reduce_relay(sent, current, chips, sections, collective_id):
    _, rows, width = sent.shape

    def kernel(sent_ref, current_ref, result_ref, carried_ref, pieces, send_sem, recv_sem,
               local_sem, relay_send, relay_recv):
        me = lax.axis_index("fsdp")
        section = lax.axis_index("section")
        chip, core = me // 2, me % 2
        barrier = pltpu.get_barrier_semaphore()
        for j in range(1, chips):
            peer = lax.rem(chip + j, chips)
            pl.semaphore_signal(barrier, 1, device_id=(section, peer * 2 + core), device_id_type=MESH)

        @pl.when(section > 0)
        def _():
            pl.semaphore_signal(barrier, 1, device_id=(section - 1, me), device_id_type=MESH)

        has_next = (sections - 1 - section + sections - 2) // (sections - 1)
        pl.semaphore_wait(barrier, chips - 1 + has_next)

        local = pltpu.make_async_copy(sent_ref.at[chip], pieces.at[chip], local_sem)
        local.start()
        copies = []
        for j in range(1, chips):
            peer = lax.rem(chip + j, chips)
            copy = pltpu.make_async_remote_copy(
                src_ref=sent_ref.at[peer],
                dst_ref=pieces.at[chip],
                send_sem=send_sem.at[j],
                recv_sem=recv_sem.at[j],
                device_id=(section, peer * 2 + core),
                device_id_type=MESH,
            )
            copy.start()
            copies.append(copy)
        local.wait()
        for copy in copies:
            copy.wait()
        mixed = pieces[0].astype(jnp.float32)
        for k in range(1, chips):
            mixed = mixed + pieces[k].astype(jnp.float32)
        result_ref[...] = (current_ref[...].astype(jnp.float32) + mixed).astype(result_ref.dtype)
        relay = pltpu.make_async_remote_copy(
            src_ref=result_ref,
            dst_ref=carried_ref,
            send_sem=relay_send,
            recv_sem=relay_recv,
            device_id=(section + 1, me),
            device_id_type=MESH,
        )

        @pl.when(section < sections - 1)
        def _():
            relay.start()
            relay.wait_send()

        @pl.when(section > 0)
        def _():
            relay.wait_recv()

    vmem = pl.BlockSpec(memory_space=pltpu.VMEM)
    return pl.pallas_call(
        kernel,
        out_shape=(
            jax.ShapeDtypeStruct((rows, width), current.dtype),
            jax.ShapeDtypeStruct((rows, width), current.dtype),
        ),
        in_specs=[pl.BlockSpec(memory_space=pl.ANY), vmem],
        out_specs=(vmem, vmem),
        scratch_shapes=[
            pltpu.VMEM((chips, rows, width), sent.dtype),
            pltpu.SemaphoreType.DMA((chips,)),
            pltpu.SemaphoreType.DMA((chips,)),
            pltpu.SemaphoreType.DMA(()),
            pltpu.SemaphoreType.DMA(()),
            pltpu.SemaphoreType.DMA(()),
        ],
        compiler_params=pltpu.CompilerParams(collective_id=collective_id, has_side_effects=True),
    )(sent, current)


def passed_along(array, axis, by):
    devices = lax.axis_size(axis)
    pairs = [(i, i + by) for i in range(devices) if 0 <= i + by < devices]
    return lax.ppermute(array, axis, pairs)


def sibling(array, axis):
    devices = lax.axis_size(axis)
    return lax.ppermute(array, axis, [(i, i ^ 1) for i in range(devices)])


def rms_norm(rows, gain_row):
    values = rows.astype(jnp.float32)
    scale = lax.rsqrt(jnp.mean(values * values, axis=-1, keepdims=True) + 1e-05)
    return (values * scale * gain_row[None, :]).astype(jnp.bfloat16)


def combine_weights(route_layer, share_layer, experts, shards):
    micro, tokens, top = route_layer.shape
    per = tokens // shards
    onehot = (route_layer[..., None] == jnp.arange(experts, dtype=route_layer.dtype)).astype(jnp.float32)
    coef = jnp.sum(onehot * share_layer[..., None], axis=2)
    return coef.reshape(micro, shards, per, experts).transpose(0, 3, 1, 2)


def expert_mix(rows, coef, gate_w, up_w, down_w):
    gate = jnp.einsum("fmd,edh->fmeh", rows, gate_w, preferred_element_type=jnp.float32)
    upward = jnp.einsum("fmd,edh->fmeh", rows, up_w, preferred_element_type=jnp.float32)
    share = jnp.transpose(coef, (1, 2, 0))[..., None]
    gated = (jax.nn.silu(gate) * upward * share).astype(jnp.bfloat16)
    shards, local, experts, hidden = gated.shape
    gated = gated.reshape(shards, local, experts * hidden)
    down = down_w.reshape(experts * hidden, down_w.shape[2])
    return jnp.einsum("fmk,kd->fmd", gated, down, preferred_element_type=jnp.float32)


def on_device(inputs, gain, w_gate, w_up, w_down, routes, shares):
    sections = lax.axis_size("section")
    shards = lax.axis_size("fsdp")
    chips = shards // 2
    section_index = lax.axis_index("section")
    core = lax.axis_index("fsdp") % 2
    micro, local, width = inputs.shape
    gain_row = gain[0]
    gate_w, up_w, down_w = w_gate[0], w_up[0], w_down[0]
    experts = gate_w.shape[0]
    chunks = 2
    per = micro * local // chunks
    coef = combine_weights(routes[0], shares[0], experts, shards)
    coef = coef.transpose(1, 2, 0, 3).reshape(experts, shards, chunks, per).transpose(2, 0, 1, 3)
    coef = coef.reshape(chunks, experts, chips, 2, per)
    coef = jnp.concatenate(
        [
            lax.dynamic_index_in_dim(coef, core, 3, keepdims=False),
            lax.dynamic_index_in_dim(coef, 1 - core, 3, keepdims=False),
        ],
        axis=2,
    )
    lanes = per * width // 128
    flat_inputs = inputs.reshape(chunks, lanes, 128)
    output = jnp.zeros_like(flat_inputs)
    carried = None
    for tick in range(chunks + sections - 1):
        position = tick - section_index
        valid = jnp.logical_and(position >= 0, position < chunks)
        clipped = jnp.clip(position, 0, chunks - 1)
        entry = lax.dynamic_index_in_dim(flat_inputs, clipped, 0, keepdims=False)
        coef_now = lax.dynamic_index_in_dim(coef, clipped, 0, keepdims=False)
        current = entry if carried is None else jnp.where(section_index == 0, entry, carried)
        normed = rms_norm(current.reshape(per, width), gain_row)
        near = exchange(normed.reshape(lanes, 128), chips, True, 0)
        rows = jnp.concatenate([near, sibling(near, "fsdp")], axis=0).reshape(shards, per, width)
        partial_value = expert_mix(rows, coef_now, gate_w, up_w, down_w)
        far_sum = sibling(partial_value[chips:].astype(jnp.bfloat16), "fsdp")
        chip_sum = partial_value[:chips] + far_sum.astype(jnp.float32)
        sent = chip_sum.astype(jnp.bfloat16).reshape(chips, lanes, 128)
        result, carried = reduce_relay(sent, current, chips, sections, 1)
        updated = lax.dynamic_update_index_in_dim(output, result, clipped, 0)
        output = jnp.where(valid, updated, output)
    return output.reshape(1, micro, local, width)


def solution(mesh):
    placed = (
        P(None, "fsdp", None),
        P("section", None),
        P("section", None, None, "fsdp"),
        P("section", None, None, "fsdp"),
        P("section", None, "fsdp", None),
        P("section", None, None, None),
        P("section", None, None, None),
    )
    return jax.shard_map(
        on_device,
        mesh=mesh,
        in_specs=placed,
        out_specs=P("section", None, "fsdp", None),
        check_vma=False,
    )
```

```python
import jax
import jax.numpy as jnp
from jax import lax
from jax.sharding import PartitionSpec as P
from jax.experimental import pallas as pl
from jax.experimental.pallas import tpu as pltpu

MESH = pl.DeviceIdType.MESH


def farthest_first(chips):
    side = int(round(chips ** 0.5))
    hops = lambda d: min(d, side - d)
    offsets = [(dx, dz) for dx in range(side) for dz in range(side) if (dx, dz) != (0, 0)]
    offsets.sort(key=lambda o: -(hops(o[0]) + hops(o[1])))
    return side, [(0, 0)] + offsets


def torus_peer(chip, j, chips):
    side, offsets = farthest_first(chips)
    dx, dz = offsets[j]
    x, z = chip // side, chip % side
    return lax.rem(x + dx, side) * side + lax.rem(z + dz, side)


def exchange(src, chips, same, collective_id):
    rows, width = src.shape[-2:]

    def kernel(src_ref, out_ref, send_sem, recv_sem, local_sem):
        me = lax.axis_index("fsdp")
        section = lax.axis_index("section")
        chip, core = me // 2, me % 2
        barrier = pltpu.get_barrier_semaphore()
        for j in range(1, chips):
            peer = torus_peer(chip, j, chips)
            pl.semaphore_signal(barrier, 1, device_id=(section, peer * 2 + core), device_id_type=MESH)
        pl.semaphore_wait(barrier, chips - 1)
        local = pltpu.make_async_copy(src_ref if same else src_ref.at[chip], out_ref.at[chip], local_sem)
        local.start()
        copies = []
        for j in range(1, chips):
            peer = torus_peer(chip, j, chips)
            copy = pltpu.make_async_remote_copy(
                src_ref=src_ref if same else src_ref.at[peer],
                dst_ref=out_ref.at[chip],
                send_sem=send_sem.at[j],
                recv_sem=recv_sem.at[j],
                device_id=(section, peer * 2 + core),
                device_id_type=MESH,
            )
            copy.start()
            copies.append(copy)
        local.wait()
        for copy in copies:
            copy.wait()

    return pl.pallas_call(
        kernel,
        out_shape=jax.ShapeDtypeStruct((chips, rows, width), src.dtype),
        in_specs=[pl.BlockSpec(memory_space=pl.ANY)],
        out_specs=pl.BlockSpec(memory_space=pl.ANY),
        scratch_shapes=[
            pltpu.SemaphoreType.DMA((chips,)),
            pltpu.SemaphoreType.DMA((chips,)),
            pltpu.SemaphoreType.DMA(()),
        ],
        compiler_params=pltpu.CompilerParams(collective_id=collective_id, has_side_effects=True),
    )(src)


def reduce_relay(sent, current, chips, sections, collective_id):
    _, rows, width = sent.shape

    def kernel(sent_ref, current_ref, result_ref, carried_ref, pieces, send_sem, recv_sem,
               local_sem, relay_send, relay_recv):
        me = lax.axis_index("fsdp")
        section = lax.axis_index("section")
        chip, core = me // 2, me % 2
        barrier = pltpu.get_barrier_semaphore()
        for j in range(1, chips):
            peer = torus_peer(chip, j, chips)
            pl.semaphore_signal(barrier, 1, device_id=(section, peer * 2 + core), device_id_type=MESH)

        @pl.when(section > 0)
        def _():
            pl.semaphore_signal(barrier, 1, device_id=(section - 1, me), device_id_type=MESH)

        has_next = (sections - 1 - section + sections - 2) // (sections - 1)
        pl.semaphore_wait(barrier, chips - 1 + has_next)

        local = pltpu.make_async_copy(sent_ref.at[chip], pieces.at[chip], local_sem)
        local.start()
        copies = []
        for j in range(1, chips):
            peer = torus_peer(chip, j, chips)
            copy = pltpu.make_async_remote_copy(
                src_ref=sent_ref.at[peer],
                dst_ref=pieces.at[chip],
                send_sem=send_sem.at[j],
                recv_sem=recv_sem.at[j],
                device_id=(section, peer * 2 + core),
                device_id_type=MESH,
            )
            copy.start()
            copies.append(copy)
        local.wait()
        for copy in copies:
            copy.wait()
        mixed = pieces[0].astype(jnp.float32)
        for k in range(1, chips):
            mixed = mixed + pieces[k].astype(jnp.float32)
        result_ref[...] = (current_ref[...].astype(jnp.float32) + mixed).astype(result_ref.dtype)
        relay = pltpu.make_async_remote_copy(
            src_ref=result_ref,
            dst_ref=carried_ref,
            send_sem=relay_send,
            recv_sem=relay_recv,
            device_id=(section + 1, me),
            device_id_type=MESH,
        )

        @pl.when(section < sections - 1)
        def _():
            relay.start()
            relay.wait_send()

        @pl.when(section > 0)
        def _():
            relay.wait_recv()

    vmem = pl.BlockSpec(memory_space=pltpu.VMEM)
    return pl.pallas_call(
        kernel,
        out_shape=(
            jax.ShapeDtypeStruct((rows, width), current.dtype),
            jax.ShapeDtypeStruct((rows, width), current.dtype),
        ),
        in_specs=[pl.BlockSpec(memory_space=pl.ANY), vmem],
        out_specs=(vmem, vmem),
        scratch_shapes=[
            pltpu.VMEM((chips, rows, width), sent.dtype),
            pltpu.SemaphoreType.DMA((chips,)),
            pltpu.SemaphoreType.DMA((chips,)),
            pltpu.SemaphoreType.DMA(()),
            pltpu.SemaphoreType.DMA(()),
            pltpu.SemaphoreType.DMA(()),
        ],
        compiler_params=pltpu.CompilerParams(collective_id=collective_id, has_side_effects=True),
    )(sent, current)


def passed_along(array, axis, by):
    devices = lax.axis_size(axis)
    pairs = [(i, i + by) for i in range(devices) if 0 <= i + by < devices]
    return lax.ppermute(array, axis, pairs)


def sibling(array, axis):
    devices = lax.axis_size(axis)
    return lax.ppermute(array, axis, [(i, i ^ 1) for i in range(devices)])


def rms_norm(rows, gain_row):
    values = rows.astype(jnp.float32)
    scale = lax.rsqrt(jnp.mean(values * values, axis=-1, keepdims=True) + 1e-05)
    return (values * scale * gain_row[None, :]).astype(jnp.bfloat16)


def combine_weights(route_layer, share_layer, experts, shards):
    micro, tokens, top = route_layer.shape
    per = tokens // shards
    onehot = (route_layer[..., None] == jnp.arange(experts, dtype=route_layer.dtype)).astype(jnp.float32)
    coef = jnp.sum(onehot * share_layer[..., None], axis=2)
    return coef.reshape(micro, shards, per, experts).transpose(0, 3, 1, 2)


def expert_mix(rows, coef, gate_w, up_w, down_w):
    gate = jnp.einsum("fmd,edh->fmeh", rows, gate_w, preferred_element_type=jnp.float32)
    upward = jnp.einsum("fmd,edh->fmeh", rows, up_w, preferred_element_type=jnp.float32)
    share = jnp.transpose(coef, (1, 2, 0))[..., None]
    gated = (jax.nn.silu(gate) * upward * share).astype(jnp.bfloat16)
    shards, local, experts, hidden = gated.shape
    gated = gated.reshape(shards, local, experts * hidden)
    down = down_w.reshape(experts * hidden, down_w.shape[2])
    return jnp.einsum("fmk,kd->fmd", gated, down, preferred_element_type=jnp.float32)


def on_device(inputs, gain, w_gate, w_up, w_down, routes, shares):
    sections = lax.axis_size("section")
    shards = lax.axis_size("fsdp")
    chips = shards // 2
    section_index = lax.axis_index("section")
    core = lax.axis_index("fsdp") % 2
    micro, local, width = inputs.shape
    gain_row = gain[0]
    gate_w, up_w, down_w = w_gate[0], w_up[0], w_down[0]
    experts = gate_w.shape[0]
    coef = combine_weights(routes[0], shares[0], experts, shards)
    coef = coef.reshape(micro, experts, chips, 2, local)
    coef = jnp.concatenate(
        [
            lax.dynamic_index_in_dim(coef, core, 3, keepdims=False),
            lax.dynamic_index_in_dim(coef, 1 - core, 3, keepdims=False),
        ],
        axis=2,
    )
    lanes = local * width // 128
    flat_inputs = inputs.reshape(micro, lanes, 128)
    output = jnp.zeros_like(flat_inputs)
    carried = None
    for tick in range(micro + sections - 1):
        position = tick - section_index
        valid = jnp.logical_and(position >= 0, position < micro)
        clipped = jnp.clip(position, 0, micro - 1)
        entry = lax.dynamic_index_in_dim(flat_inputs, clipped, 0, keepdims=False)
        coef_now = lax.dynamic_index_in_dim(coef, clipped, 0, keepdims=False)
        current = entry if carried is None else jnp.where(section_index == 0, entry, carried)
        normed = rms_norm(current.reshape(local, width), gain_row)
        near = exchange(normed.reshape(lanes, 128), chips, True, 0)
        rows = jnp.concatenate([near, sibling(near, "fsdp")], axis=0).reshape(shards, local, width)
        partial_value = expert_mix(rows, coef_now, gate_w, up_w, down_w)
        far_sum = sibling(partial_value[chips:].astype(jnp.bfloat16), "fsdp")
        chip_sum = partial_value[:chips] + far_sum.astype(jnp.float32)
        sent = chip_sum.astype(jnp.bfloat16).reshape(chips, lanes, 128)
        result, carried = reduce_relay(sent, current, chips, sections, 1)
        updated = lax.dynamic_update_index_in_dim(output, result, clipped, 0)
        output = jnp.where(valid, updated, output)
    return output.reshape(1, micro, local, width)


def solution(mesh):
    placed = (
        P(None, "fsdp", None),
        P("section", None),
        P("section", None, None, "fsdp"),
        P("section", None, None, "fsdp"),
        P("section", None, "fsdp", None),
        P("section", None, None, None),
        P("section", None, None, None),
    )
    return jax.shard_map(
        on_device,
        mesh=mesh,
        in_specs=placed,
        out_specs=P("section", None, "fsdp", None),
        check_vma=False,
    )
```

```python
import jax
import jax.numpy as jnp
from jax import lax
from jax.sharding import PartitionSpec as P
from jax.experimental import pallas as pl
from jax.experimental.pallas import tpu as pltpu

MESH = pl.DeviceIdType.MESH


def farthest_first(chips):
    side = int(round(chips ** 0.5))
    hops = lambda d: min(d, side - d)
    offsets = [(dx, dz) for dx in range(side) for dz in range(side) if (dx, dz) != (0, 0)]
    offsets.sort(key=lambda o: -(hops(o[0]) + hops(o[1])))
    return side, [(0, 0)] + offsets


def torus_peer(chip, j, chips):
    side, offsets = farthest_first(chips)
    dx, dz = offsets[j]
    x, z = chip // side, chip % side
    return lax.rem(x + dx, side) * side + lax.rem(z + dz, side)


def exchange(src, chips, same, collective_id):
    rows, width = src.shape[-2:]

    def kernel(src_ref, out_ref, send_sem, recv_sem, local_sem):
        me = lax.axis_index("fsdp")
        section = lax.axis_index("section")
        chip, core = me // 2, me % 2
        barrier = pltpu.get_barrier_semaphore()
        for j in range(1, chips):
            peer = torus_peer(chip, j, chips)
            pl.semaphore_signal(barrier, 1, device_id=(section, peer * 2 + core), device_id_type=MESH)
        pl.semaphore_wait(barrier, chips - 1)
        local = pltpu.make_async_copy(src_ref if same else src_ref.at[chip], out_ref.at[chip], local_sem)
        copies = []
        for j in range(1, chips):
            peer = torus_peer(chip, j, chips)
            copy = pltpu.make_async_remote_copy(
                src_ref=src_ref if same else src_ref.at[peer],
                dst_ref=out_ref.at[chip],
                send_sem=send_sem.at[j],
                recv_sem=recv_sem.at[j],
                device_id=(section, peer * 2 + core),
                device_id_type=MESH,
            )
            copy.start()
            copies.append(copy)
        local.start()
        local.wait()
        for copy in copies:
            copy.wait()

    return pl.pallas_call(
        kernel,
        out_shape=jax.ShapeDtypeStruct((chips, rows, width), src.dtype),
        in_specs=[pl.BlockSpec(memory_space=pl.ANY)],
        out_specs=pl.BlockSpec(memory_space=pl.ANY),
        scratch_shapes=[
            pltpu.SemaphoreType.DMA((chips,)),
            pltpu.SemaphoreType.DMA((chips,)),
            pltpu.SemaphoreType.DMA(()),
        ],
        compiler_params=pltpu.CompilerParams(collective_id=collective_id, has_side_effects=True),
    )(src)


def reduce_relay(sent, current, chips, sections, collective_id):
    _, rows, width = sent.shape

    def kernel(sent_ref, current_ref, result_ref, carried_ref, pieces, send_sem, recv_sem,
               local_sem, relay_send, relay_recv):
        me = lax.axis_index("fsdp")
        section = lax.axis_index("section")
        chip, core = me // 2, me % 2
        barrier = pltpu.get_barrier_semaphore()
        for j in range(1, chips):
            peer = torus_peer(chip, j, chips)
            pl.semaphore_signal(barrier, 1, device_id=(section, peer * 2 + core), device_id_type=MESH)

        @pl.when(section > 0)
        def _():
            pl.semaphore_signal(barrier, 1, device_id=(section - 1, me), device_id_type=MESH)

        has_next = (sections - 1 - section + sections - 2) // (sections - 1)
        pl.semaphore_wait(barrier, chips - 1 + has_next)

        local = pltpu.make_async_copy(sent_ref.at[chip], pieces.at[chip], local_sem)
        copies = []
        for j in range(1, chips):
            peer = torus_peer(chip, j, chips)
            copy = pltpu.make_async_remote_copy(
                src_ref=sent_ref.at[peer],
                dst_ref=pieces.at[chip],
                send_sem=send_sem.at[j],
                recv_sem=recv_sem.at[j],
                device_id=(section, peer * 2 + core),
                device_id_type=MESH,
            )
            copy.start()
            copies.append(copy)
        local.start()
        local.wait()
        for copy in copies:
            copy.wait()
        mixed = pieces[0].astype(jnp.float32)
        for k in range(1, chips):
            mixed = mixed + pieces[k].astype(jnp.float32)
        result_ref[...] = (current_ref[...].astype(jnp.float32) + mixed).astype(result_ref.dtype)
        relay = pltpu.make_async_remote_copy(
            src_ref=result_ref,
            dst_ref=carried_ref,
            send_sem=relay_send,
            recv_sem=relay_recv,
            device_id=(section + 1, me),
            device_id_type=MESH,
        )

        @pl.when(section < sections - 1)
        def _():
            relay.start()
            relay.wait_send()

        @pl.when(section > 0)
        def _():
            relay.wait_recv()

    vmem = pl.BlockSpec(memory_space=pltpu.VMEM)
    return pl.pallas_call(
        kernel,
        out_shape=(
            jax.ShapeDtypeStruct((rows, width), current.dtype),
            jax.ShapeDtypeStruct((rows, width), current.dtype),
        ),
        in_specs=[pl.BlockSpec(memory_space=pl.ANY), vmem],
        out_specs=(vmem, vmem),
        scratch_shapes=[
            pltpu.VMEM((chips, rows, width), sent.dtype),
            pltpu.SemaphoreType.DMA((chips,)),
            pltpu.SemaphoreType.DMA((chips,)),
            pltpu.SemaphoreType.DMA(()),
            pltpu.SemaphoreType.DMA(()),
            pltpu.SemaphoreType.DMA(()),
        ],
        compiler_params=pltpu.CompilerParams(collective_id=collective_id, has_side_effects=True),
    )(sent, current)


def passed_along(array, axis, by):
    devices = lax.axis_size(axis)
    pairs = [(i, i + by) for i in range(devices) if 0 <= i + by < devices]
    return lax.ppermute(array, axis, pairs)


def sibling(array, axis):
    devices = lax.axis_size(axis)
    return lax.ppermute(array, axis, [(i, i ^ 1) for i in range(devices)])


def rms_norm(rows, gain_row):
    values = rows.astype(jnp.float32)
    scale = lax.rsqrt(jnp.mean(values * values, axis=-1, keepdims=True) + 1e-05)
    return (values * scale * gain_row[None, :]).astype(jnp.bfloat16)


def combine_weights(route_layer, share_layer, experts, shards):
    micro, tokens, top = route_layer.shape
    per = tokens // shards
    onehot = (route_layer[..., None] == jnp.arange(experts, dtype=route_layer.dtype)).astype(jnp.float32)
    coef = jnp.sum(onehot * share_layer[..., None], axis=2)
    return coef.reshape(micro, shards, per, experts).transpose(0, 3, 1, 2)


def expert_mix(rows, coef, gate_w, up_w, down_w):
    gate = jnp.einsum("fmd,edh->fmeh", rows, gate_w, preferred_element_type=jnp.float32)
    upward = jnp.einsum("fmd,edh->fmeh", rows, up_w, preferred_element_type=jnp.float32)
    share = jnp.transpose(coef, (1, 2, 0))[..., None]
    gated = (jax.nn.silu(gate) * upward * share).astype(jnp.bfloat16)
    shards, local, experts, hidden = gated.shape
    gated = gated.reshape(shards, local, experts * hidden)
    down = down_w.reshape(experts * hidden, down_w.shape[2])
    return jnp.einsum("fmk,kd->fmd", gated, down, preferred_element_type=jnp.float32)


def on_device(inputs, gain, w_gate, w_up, w_down, routes, shares):
    sections = lax.axis_size("section")
    shards = lax.axis_size("fsdp")
    chips = shards // 2
    section_index = lax.axis_index("section")
    core = lax.axis_index("fsdp") % 2
    micro, local, width = inputs.shape
    gain_row = gain[0]
    gate_w, up_w, down_w = w_gate[0], w_up[0], w_down[0]
    experts = gate_w.shape[0]
    coef = combine_weights(routes[0], shares[0], experts, shards)
    coef = coef.reshape(micro, experts, chips, 2, local)
    coef = jnp.concatenate(
        [
            lax.dynamic_index_in_dim(coef, core, 3, keepdims=False),
            lax.dynamic_index_in_dim(coef, 1 - core, 3, keepdims=False),
        ],
        axis=2,
    )
    lanes = local * width // 128
    flat_inputs = inputs.reshape(micro, lanes, 128)
    output = jnp.zeros_like(flat_inputs)
    carried = None
    for tick in range(micro + sections - 1):
        position = tick - section_index
        valid = jnp.logical_and(position >= 0, position < micro)
        clipped = jnp.clip(position, 0, micro - 1)
        entry = lax.dynamic_index_in_dim(flat_inputs, clipped, 0, keepdims=False)
        coef_now = lax.dynamic_index_in_dim(coef, clipped, 0, keepdims=False)
        current = entry if carried is None else jnp.where(section_index == 0, entry, carried)
        normed = rms_norm(current.reshape(local, width), gain_row)
        near = exchange(normed.reshape(lanes, 128), chips, True, 0)
        rows = jnp.concatenate([near, sibling(near, "fsdp")], axis=0).reshape(shards, local, width)
        partial_value = expert_mix(rows, coef_now, gate_w, up_w, down_w)
        far_sum = sibling(partial_value[chips:].astype(jnp.bfloat16), "fsdp")
        chip_sum = partial_value[:chips] + far_sum.astype(jnp.float32)
        sent = chip_sum.astype(jnp.bfloat16).reshape(chips, lanes, 128)
        result, carried = reduce_relay(sent, current, chips, sections, 1)
        updated = lax.dynamic_update_index_in_dim(output, result, clipped, 0)
        output = jnp.where(valid, updated, output)
    return output.reshape(1, micro, local, width)


def solution(mesh):
    placed = (
        P(None, "fsdp", None),
        P("section", None),
        P("section", None, None, "fsdp"),
        P("section", None, None, "fsdp"),
        P("section", None, "fsdp", None),
        P("section", None, None, None),
        P("section", None, None, None),
    )
    return jax.shard_map(
        on_device,
        mesh=mesh,
        in_specs=placed,
        out_specs=P("section", None, "fsdp", None),
        check_vma=False,
    )
```
